256 devices in a mesh: grid: 64 (over x, z_lo, y), band: 4 (over z_hi, core).
Axes of the slice: x: 4, y: 4, z: 8 (z_hi: 2, z_lo: 4; z = z_hi * 4 + z_lo), core: 2. Of those that a mesh axis runs over, the one named last changes fastest.
Arguments:
- coefficients: float32 [2, 4, 1048576], P(None, 'band', 'grid'), may hold values from -60 to 60
- index_map: int32 [1048576], P('grid'), may hold values from 0 to 110591, as said below
- potential: float32 [192, 36864], P('grid'), may hold values from 0.5 to 2.5
Outputs:
- subspace: float32 [2, 4, 4], P(None, None, 'band')
- residual: float32 [2, 4, 1048576], P(None, 'band', 'grid')
The draws below stay inside these ranges and needn't reach their ends.
Inputs may be any that keep to these rules, and one draw needn't show every extreme that they name: `index_map`: entries 16384 * g to 16384 * (g + 1) - 1 name distinct cells m = ga * 3 * 192 + (gb % 3) * 192 + gc of grid device g's slab of frequency planes, all with fa * fa + fc * fc < 2304, where fa and fc are ga and gc folded into -96 to 95.
All inputs are finite; a program needn't handle non-finite values.
Results may differ from the reference program's by a relative error of at most 0.000062.
Values sent between devices are 32-bit elements; how exact they have to be, the bound alone decides.
A program may use at most 64 MiB of HBM per device.

```python
import math
import jax
import jax.numpy as jnp
from jax import lax

N = 192
NPW_DEV = 16384
SLAB = 3
BANDS = 4
NPW = 1048576
N_GRID = 64


def draw_coefficients(key, part):
    key_list = jax.random.split(key, 4)
    common = jnp.clip(jax.random.normal(key_list[0], (2, NPW), jnp.float32), -6.0, 6.0)
    single = jnp.clip(jax.random.normal(key_list[1], (2, BANDS, NPW), jnp.float32), -6.0, 6.0)
    log_low = math.log(0.3)
    log_high = math.log(3.0)
    shared_weight = 0.6
    own_weight = 0.8
    spread = jnp.exp(jax.random.uniform(key_list[2], (NPW,), jnp.float32, log_low, log_high))
    band_gain = jnp.exp(jax.random.uniform(key_list[3], (BANDS,), jnp.float32, math.log(0.5), math.log(2.0)))
    mixed = shared_weight * common[:, None, :] + own_weight * single
    return (band_gain[None, :, None] * spread[None, None, :] * mixed).astype(jnp.float32)


def draw_index_map(key, part):
    planes = N // N_GRID
    cell_total = N * planes * N
    quarter = N // 4
    cell_ids = jnp.arange(cell_total, dtype=jnp.int32)
    row_freq = cell_ids // (planes * N)
    col_freq = cell_ids % N
    row_fold = jnp.where(row_freq < N // 2, row_freq, row_freq - N)
    col_fold = jnp.where(col_freq < N // 2, col_freq, col_freq - N)
    inside = row_fold * row_fold + col_fold * col_fold < quarter * quarter

    def pick(device):
        order_key = jax.random.fold_in(key, device)
        shuffled = jax.random.permutation(order_key, cell_total).astype(jnp.int32)
        outside = jnp.where(inside[shuffled], 0, 1).astype(jnp.int32)
        forced = jnp.logical_or(shuffled == 0, shuffled == cell_total - 1)
        priority = jnp.where(forced, -1, outside).astype(jnp.int32)
        ranking = jnp.argsort(priority, stable=True)
        return shuffled[ranking[:NPW_DEV]]
    chosen = lax.map(pick, jnp.arange(N_GRID, dtype=jnp.int32))
    return chosen.reshape(-1).astype(jnp.int32)


def level_of(stream_key, shape, shards, smallest, high):
    loudness, own = 1.0, jax.random.fold_in(stream_key, 6)
    for dim, shards_of in shards:
        draws = jnp.exp(jax.random.uniform(jax.random.fold_in(own, dim), (shards_of,), jnp.float32, smallest / len(shards), high / len(shards)))
        loudness = loudness * jnp.repeat(draws, shape[dim] // shards_of).reshape([-1 if axis == dim else 1 for axis in range(len(shape))])
    return loudness


def setup_inputs(seed: int = 0) -> dict:
    seeds = jax.random.split(jax.random.key(seed), 4)
    return {
        "coefficients": draw_coefficients(jax.random.fold_in(seeds[3], 71), 0),
        "index_map": draw_index_map(jax.random.fold_in(seeds[3], 71), 0),
        "potential": jnp.clip(0.5 + 2.0 * jax.random.uniform(seeds[2], (N, N * N), jnp.float32) ** level_of(seeds[2], (N, N * N), ((0, 64),), -0.2, 0.2), 0.5, 2.5),
    }


def reference(coefficients, index_map, potential):
    position = jnp.arange(NPW, dtype=jnp.int32)
    owner = position // NPW_DEV
    row_freq = index_map // (SLAB * N)
    mid_freq = owner * SLAB + (index_map // N) % SLAB
    col_freq = index_map % N
    flat_cell = (row_freq * N + mid_freq) * N + col_freq
    cube_pot = potential.reshape(N, N, N)

    def apply_band(band_pair):
        real_part = jnp.zeros((N * N * N,), coefficients.dtype).at[flat_cell].set(band_pair[0])
        imag_part = jnp.zeros((N * N * N,), coefficients.dtype).at[flat_cell].set(band_pair[1])
        spectrum = lax.complex(real_part, imag_part).reshape(N, N, N)
        field = jnp.fft.ifftn(spectrum)
        applied = jnp.fft.fftn(cube_pot * field).reshape(-1)[flat_cell]
        return jnp.real(applied), jnp.imag(applied)

    stacked = jnp.transpose(coefficients, (1, 0, 2))
    applied_re, applied_im = lax.map(apply_band, stacked)
    coef_re = coefficients[0]
    coef_im = coefficients[1]
    highest = lax.Precision.HIGHEST
    sub_re = (jnp.dot(coef_re, applied_re.T, precision=highest) + jnp.dot(coef_im, applied_im.T, precision=highest)) / NPW
    sub_im = (jnp.dot(coef_re, applied_im.T, precision=highest) - jnp.dot(coef_im, applied_re.T, precision=highest)) / NPW
    resid_re = applied_re - (jnp.dot(sub_re.T, coef_re, precision=highest) - jnp.dot(sub_im.T, coef_im, precision=highest))
    resid_im = applied_im - (jnp.dot(sub_im.T, coef_re, precision=highest) + jnp.dot(sub_re.T, coef_im, precision=highest))
    return jnp.stack([sub_re, sub_im]), jnp.stack([resid_re, resid_im])
```

```python
import functools
import math

import jax
import jax.numpy as jnp
import ml_dtypes
import numpy as np
from jax import lax
from jax.experimental import pallas as pl
from jax.experimental.pallas import tpu as pltpu
from jax.sharding import PartitionSpec as P

N = 192
HALF = 96
PARTS = 64
SLAB = 3
KS = 8
LA, LB = 384, 256
LANES = LA + LB
F32, BF16 = jnp.float32, jnp.bfloat16
MESH = pl.DeviceIdType.MESH
VMEM = pltpu.VMEM


def split(table):
    hi = table.astype(np.float32).astype(ml_dtypes.bfloat16)
    lo = (table - hi.astype(np.float64)).astype(np.float32).astype(ml_dtypes.bfloat16)
    return hi, lo


def make_tables():
    turn = 2.0 * math.pi / N
    fold = np.arange(HALF)
    freq = np.where(fold < HALF // 2, fold, fold + HALF)
    plane = 3 * np.arange(PARTS)[None, :] + np.arange(SLAB)[:, None]
    plane = plane.reshape(-1)
    cells = np.arange(N)
    angle = turn * (plane[:, None] * freq[None, :] % N)
    first = np.concatenate([np.cos(angle), np.sin(angle)], 0)
    angle = turn * (cells[:, None] * plane[None, :] % N)
    middle = np.concatenate([np.cos(angle), np.sin(angle)], 0)
    lane_freq = np.zeros(256, np.int64)
    kind = np.full(256, -1)
    lane_freq[0:64], kind[0:64] = freq[:64], 0
    lane_freq[64:128], kind[64:128] = freq[:64], 1
    lane_freq[128:160], kind[128:160] = freq[64:], 0
    lane_freq[192:224], kind[192:224] = freq[64:], 1
    angle = turn * (lane_freq[:, None] * cells[None, :] % N)
    cos, sin = np.cos(angle), np.sin(angle)
    re, im = (kind == 0)[:, None], (kind == 1)[:, None]
    to_re = re * cos - im * sin
    to_im = re * sin + im * cos
    norm = 1.0 / float(N) ** 3
    from_re = (re * cos - im * sin).T * norm
    from_im = (re * sin + im * cos).T * norm
    angle = turn * (plane[:, None] * cells[None, :] % N)
    middle_back = np.concatenate([np.cos(angle), np.sin(angle)], 0)
    angle = turn * (freq[:, None] * plane[None, :] % N)
    first_back = np.concatenate([np.cos(angle), np.sin(angle)], 0)
    tables = (first, middle, to_re, to_im, from_re, from_im, middle_back, first_back)
    return [np.stack(split(table)) for table in tables]


def halves(x):
    hi = x.astype(BF16)
    return hi, (x - hi.astype(F32)).astype(BF16)


def dot(a, b):
    return jnp.dot(a, b, preferred_element_type=F32)


def dot_left(table, hi, lo):
    return dot(table[0], hi) + dot(table[1], hi) + dot(table[0], lo)


def dot_right(hi, lo, table):
    return dot(hi, table[0]) + dot(lo, table[0]) + dot(hi, table[1])


def groups(x):
    return [x[:, 128 * g : 128 * g + 128] for g in range(x.shape[1] // 128)]


def combine(both, sign):
    rows = both.shape[0] // 2
    lane = lax.broadcasted_iota(jnp.int32, (rows, 128), 1)
    factor = jnp.where(lane < 64, -sign, sign).astype(F32)
    parts = [
        c + factor * pltpu.roll(s, 64, 1)
        for c, s in zip(groups(both[:rows]), groups(both[rows:]))
    ]
    return jnp.concatenate(parts, 1)


def kernel(
    index_ref,
    coef_ref,
    pot_ref,
    first,
    middle,
    to_re,
    to_im,
    from_re,
    from_im,
    middle_back,
    first_back,
    sub_ref,
    res_ref,
    row_key,
    col_key,
    coef_hi,
    coef_lo,
    acc,
    send1,
    recv1,
    send2,
    recv2,
    trash,
    table,
    all_coef,
    applied,
    part,
    parts_in,
    send_sem,
    recv_sem,
    band_send,
    band_recv,
    own_sem,
):
    me = lax.axis_index("grid")
    band = lax.axis_index("band")
    sibling = band + 1 - 2 * lax.rem(band, 2)
    across = lax.rem(band + 2, 4)
    opposite = lax.rem(sibling + 2, 4)

    barrier = pltpu.get_barrier_semaphore()

    def greet(i, carry):
        peer = lax.rem(me + i, PARTS)
        pl.semaphore_signal(barrier, inc=1, device_id={"grid": peer}, device_id_type=MESH)
        return carry

    lax.fori_loop(1, PARTS, greet, 0)
    pl.semaphore_signal(barrier, inc=1, device_id={"band": sibling}, device_id_type=MESH)
    pl.semaphore_signal(barrier, inc=1, device_id={"band": across}, device_id_type=MESH)

    cell = index_ref[...].astype(F32)
    line = jnp.floor((cell + 0.5) * (1.0 / N))
    gc = cell - N * line
    ga = jnp.floor((cell + 0.5) * (1.0 / (SLAB * N)))
    slab = line - SLAB * ga
    row_key[...] = slab * HALF + jnp.where(ga < HALF, ga, ga - HALF)
    col_key[...] = jnp.where(gc < HALF, gc, gc - HALF)
    coef = coef_ref[...]
    coef_hi[...] = coef.astype(BF16).astype(F32)
    coef_lo[...] = coef - coef.astype(BF16).astype(F32)
    acc[...] = jnp.zeros_like(acc)

    iota96 = lax.broadcasted_iota(jnp.int32, (HALF, 128), 0).astype(F32)
    iota96h = iota96.astype(BF16)
    one, zero = jnp.ones((), BF16), jnp.zeros((), BF16)
    zero32 = jnp.zeros((32, 128), BF16)

    def wide(x):
        return jnp.broadcast_to(x.astype(BF16), (HALF, 128))

    def row_hot(i):
        pieces = []
        for s in range(KS):
            key = row_key[pl.ds(i * KS + s, 1), :]
            pieces.append(
                jnp.concatenate(
                    [jnp.where(iota96h == wide(key - HALF * p), one, zero) for p in range(SLAB)], 0
                )
            )
        return jnp.concatenate(pieces, 1)

    def scatter_step(i, carry):
        pieces = []
        for s in range(KS):
            row = pl.ds(i * KS + s, 1)
            mask = iota96h == wide(col_key[row, :])
            blocks = []
            for ref in (coef_hi, coef_lo):
                re = jnp.where(mask, wide(ref[0, row, :]), zero)
                im = jnp.where(mask, wide(ref[1, row, :]), zero)
                blocks += [re[:64], im[:64], re[64:], zero32, im[64:], zero32]
            pieces.append(jnp.concatenate(blocks, 0))
        acc[...] += lax.dot_general(
            row_hot(i),
            jnp.concatenate(pieces, 1),
            (((1,), (1,)), ((), ())),
            preferred_element_type=F32,
        )
        return carry

    steps = 128 // KS
    lax.fori_loop(0, 4, scatter_step, 0)
    pl.semaphore_wait(barrier, PARTS - 1 + 2)

    def band_copy(src, dst, slot, to):
        return pltpu.make_async_remote_copy(
            src_ref=src,
            dst_ref=dst,
            send_sem=band_send.at[slot],
            recv_sem=band_recv.at[slot],
            device_id={"band": to},
            device_id_type=MESH,
        )

    to_across = band_copy(coef_ref, all_coef.at[band], 0, across)
    to_sibling = band_copy(coef_ref, all_coef.at[band], 1, sibling)
    keep = pltpu.make_async_copy(coef_ref, all_coef.at[band], own_sem)
    to_across.start()
    to_sibling.start()
    keep.start()
    lax.fori_loop(4, steps, scatter_step, 0)

    def exchange(src, dst, lanes, slot):
        def one_copy(i, carry):
            peer = lax.rem(me + i, PARTS)
            pltpu.make_async_remote_copy(
                src_ref=src.at[:, peer, lanes],
                dst_ref=dst.at[:, me, lanes],
                send_sem=send_sem.at[slot],
                recv_sem=recv_sem.at[slot],
                device_id={"grid": peer},
                device_id_type=MESH,
            ).start()
            return carry

        lax.fori_loop(1, PARTS, one_copy, 0)
        pltpu.make_async_copy(src.at[:, me, lanes], dst.at[:, me, lanes], recv_sem.at[slot]).start()
        pltpu.make_async_copy(
            src.at[:, me, lanes], trash.at[slot, :, 0, lanes], send_sem.at[slot]
        ).start()

    def arrive(src, dst, lanes, slot):
        pltpu.make_async_copy(src.at[:, :, lanes], dst.at[:, :, lanes], recv_sem.at[slot]).wait()

    def sent(src, dst, lanes, slot):
        pltpu.make_async_copy(src.at[:, :, lanes], dst.at[:, :, lanes], send_sem.at[slot]).wait()

    lanes_a, lanes_b = pl.ds(0, LA), pl.ds(LA, LB)

    def spectrum(offset):
        a = [acc[HALF * p : HALF * p + HALF, offset : offset + 128] for p in range(SLAB)]
        b = [acc[HALF * p : HALF * p + HALF, offset + 128 : offset + 256] for p in range(SLAB)]
        return (
            jnp.concatenate(a, 1).astype(BF16),
            jnp.concatenate([b[0] + pltpu.roll(b[1], 32, 1), b[2]], 1).astype(BF16),
        )

    hi_a, hi_b = spectrum(0)
    lo_a, lo_b = spectrum(256)
    out_a = combine(dot_left(first, hi_a, lo_a), 1.0)
    for j in range(SLAB):
        send1[j, :, 0:LA] = out_a[PARTS * j : PARTS * j + PARTS]
    exchange(send1, recv1, lanes_a, 0)
    out_b = combine(dot_left(first, hi_b, lo_b), 1.0)
    for j in range(SLAB):
        send1[j, :, LA:LANES] = out_b[PARTS * j : PARTS * j + PARTS]
    exchange(send1, recv1, lanes_b, 1)

    band_copy(coef_ref, all_coef.at[across], 0, across).wait_recv()
    onward = band_copy(all_coef.at[across], all_coef.at[across], 2, sibling)
    onward.start()

    arrive(send1, recv1, lanes_a, 0)
    arrive(send1, recv1, lanes_b, 1)

    def middle_step(j, carry):
        x = recv1[j]
        a = jnp.concatenate([x[:, 0:128], x[:, 128:256], x[:, 256:384]], 0)
        b = jnp.concatenate([x[:, 384:512], pltpu.roll(x[:, 384:512], 96, 1), x[:, 512:640]], 0)
        x = combine(dot_left(middle, *halves(jnp.concatenate([a, b], 1))), 1.0)
        hi, lo = halves(x)
        pot = pot_ref[j]
        field_re = dot_right(hi, lo, to_re) * pot
        field_im = dot_right(hi, lo, to_im) * pot
        x = dot_right(*halves(field_re), from_re) + dot_right(*halves(field_im), from_im)
        x = combine(dot_left(middle_back, *halves(x)), -1.0)
        for p in range(SLAB):
            send2[j, :, 128 * p : 128 * p + 128] = x[PARTS * p : PARTS * p + PARTS, 0:128]
        send2[j, :, 384:512] = x[0:64, 128:256] + pltpu.roll(x[64:128, 128:256], 32, 1)
        send2[j, :, 512:640] = x[128:192, 128:256]
        return carry

    lax.fori_loop(0, SLAB, middle_step, 0)
    exchange(send2, recv2, lanes_a, 2)
    exchange(send2, recv2, lanes_b, 3)
    arrive(send2, recv2, lanes_a, 2)
    arrive(send2, recv2, lanes_b, 3)

    x = recv2[...].reshape(N, LANES)
    x = combine(dot_left(first_back, *halves(x)), -1.0)
    b0 = x[:, 384:512]
    x = jnp.concatenate(
        [
            jnp.concatenate([x[:, 0:128], x[:, 128:256], x[:, 256:384]], 0),
            jnp.concatenate([b0, pltpu.roll(b0, 96, 1), x[:, 512:640]], 0),
        ],
        1,
    ).T
    x = jnp.concatenate([x[0:64], x[128:160], x[64:128], x[192:224]], 0)
    hi, lo = halves(x)
    table[0] = hi
    table[1] = lo

    def gather_step(i, carry):
        hot = row_hot(i)
        found = dot(table[0], hot) + dot(table[1], hot)
        for s in range(KS):
            row = pl.ds(i * KS + s, 1)
            mask = iota96 == jnp.broadcast_to(col_key[row, :], (HALF, 128))
            here = found[:, 128 * s : 128 * s + 128]
            for k in range(2):
                kept = jnp.where(mask, here[HALF * k : HALF * k + HALF], 0.0)
                applied[k, row, :] = kept.reshape(12, 8, 128).sum(0).sum(0, keepdims=True)
        return carry

    lax.fori_loop(0, steps, gather_step, 0)

    band_copy(coef_ref, all_coef.at[sibling], 1, sibling).wait_recv()
    band_copy(coef_ref, all_coef.at[opposite], 2, sibling).wait_recv()
    keep.wait()

    h_re, h_im = applied[0], applied[1]
    sums = []
    for i in range(4):
        c_re, c_im = all_coef[i, 0], all_coef[i, 1]
        sums.append((c_re * h_re + c_im * h_im, c_re * h_im - c_im * h_re))
    lanes = [s[0].sum(0, keepdims=True) for s in sums] + [s[1].sum(0, keepdims=True) for s in sums]
    total = jnp.concatenate(lanes, 0).sum(1, keepdims=True)
    eye = lax.broadcasted_iota(jnp.int32, (8, 128), 0) == lax.broadcasted_iota(
        jnp.int32, (8, 128), 1
    )
    line = jnp.where(eye, jnp.broadcast_to(total, (8, 128)), 0.0).sum(0, keepdims=True)
    part[...] = jnp.broadcast_to(line.reshape(1, 1, 128), part.shape)

    def share(i, carry):
        peer = lax.rem(me + i, PARTS)
        pltpu.make_async_remote_copy(
            src_ref=part.at[:, 0],
            dst_ref=parts_in.at[:, me],
            send_sem=send_sem.at[4],
            recv_sem=recv_sem.at[4],
            device_id={"grid": peer},
            device_id_type=MESH,
        ).start()
        return carry

    lax.fori_loop(1, PARTS, share, 0)
    pltpu.make_async_copy(part.at[:, 0], parts_in.at[:, me], recv_sem.at[4]).start()
    pltpu.make_async_copy(part.at[:, 0], trash.at[4, pl.ds(0, 1), 0, pl.ds(0, 128)], send_sem.at[4]).start()
    pltpu.make_async_copy(part, parts_in, recv_sem.at[4]).wait()

    line = parts_in[0].sum(0, keepdims=True) * (1.0 / (PARTS * 16384))
    sub_ref[...] = jnp.broadcast_to(line, (8, 128))
    r_re, r_im = h_re, h_im
    for i in range(4):
        s_re = jnp.broadcast_to(line[:, i : i + 1], (128, 128))
        s_im = jnp.broadcast_to(line[:, i + 4 : i + 5], (128, 128))
        c_re, c_im = all_coef[i, 0], all_coef[i, 1]
        r_re = r_re - (c_re * s_re - c_im * s_im)
        r_im = r_im - (c_re * s_im + c_im * s_re)
    res_ref[0] = r_re
    res_ref[1] = r_im

    sent(send1, recv1, lanes_a, 0)
    sent(send1, recv1, lanes_b, 1)
    sent(send2, recv2, lanes_a, 2)
    sent(send2, recv2, lanes_b, 3)
    pltpu.make_async_copy(part, parts_in, send_sem.at[4]).wait()
    to_across.wait_send()
    to_sibling.wait_send()
    onward.wait_send()


def local(coefficients, index_map, potential):
    tables = [jnp.asarray(t) for t in make_tables()]
    coef = coefficients.reshape(2, 128, 128)
    index = index_map.reshape(128, 128)
    pot = potential.reshape(SLAB, N, N)
    field = VMEM((SLAB, PARTS, LANES), F32)
    sub, res = pl.pallas_call(
        kernel,
        out_shape=(
            jax.ShapeDtypeStruct((8, 128), F32),
            jax.ShapeDtypeStruct((2, 128, 128), F32),
        ),
        in_specs=[pl.BlockSpec(memory_space=VMEM)] * (3 + len(tables)),
        out_specs=[pl.BlockSpec(memory_space=VMEM)] * 2,
        scratch_shapes=[
            VMEM((128, 128), F32),
            VMEM((128, 128), F32),
            VMEM((2, 128, 128), F32),
            VMEM((2, 128, 128), F32),
            VMEM((SLAB * HALF, 512), F32),
            field,
            field,
            field,
            field,
            VMEM((5, SLAB, 1, LANES), F32),
            VMEM((2, N, SLAB * HALF), BF16),
            VMEM((4, 2, 128, 128), F32),
            VMEM((2, 128, 128), F32),
            VMEM((1, PARTS, 128), F32),
            VMEM((1, PARTS, 128), F32),
            pltpu.SemaphoreType.DMA((5,)),
            pltpu.SemaphoreType.DMA((5,)),
            pltpu.SemaphoreType.DMA((3,)),
            pltpu.SemaphoreType.DMA((3,)),
            pltpu.SemaphoreType.DMA,
        ],
        compiler_params=pltpu.CompilerParams(
            collective_id=0, has_side_effects=True, vmem_limit_bytes=48 << 20
        ),
        name="apply_potential",
    )(index, coef, pot, *tables)
    return sub[0, :8].reshape(2, 4, 1), res.reshape(2, 1, 16384)


def solution(mesh):
    return jax.shard_map(
        local,
        mesh=mesh,
        in_specs=(P(None, "band", "grid"), P("grid"), P("grid", None)),
        out_specs=(P(None, None, "band"), P(None, "band", "grid")),
        check_vma=False,
    )
```

```python
import functools
import math

import jax
import jax.numpy as jnp
import ml_dtypes
import numpy as np
from jax import lax
from jax.experimental import pallas as pl
from jax.experimental.pallas import tpu as pltpu
from jax.sharding import PartitionSpec as P

N = 192
HALF = 96
PARTS = 64
SLAB = 3
KS = 16
LA, LB = 384, 256
LANES = LA + LB
F32, BF16 = jnp.float32, jnp.bfloat16
MESH = pl.DeviceIdType.MESH
VMEM = pltpu.VMEM


def split(table):
    hi = table.astype(np.float32).astype(ml_dtypes.bfloat16)
    lo = (table - hi.astype(np.float64)).astype(np.float32).astype(ml_dtypes.bfloat16)
    return hi, lo


def make_tables():
    turn = 2.0 * math.pi / N
    fold = np.arange(HALF)
    freq = np.where(fold < HALF // 2, fold, fold + HALF)
    plane = 3 * np.arange(PARTS)[None, :] + np.arange(SLAB)[:, None]
    plane = plane.reshape(-1)
    cells = np.arange(N)
    paired = np.concatenate([cells[0::2], cells[1::2]])
    angle = turn * (plane[:, None] * freq[None, :] % N)
    first = np.concatenate([np.cos(angle), np.sin(angle)], 0)
    angle = turn * (paired[:, None] * plane[None, :] % N)
    middle = np.concatenate([np.cos(angle), np.sin(angle)], 0)
    lane_freq = np.zeros(256, np.int64)
    kind = np.full(256, -1)
    lane_freq[0:64], kind[0:64] = freq[:64], 0
    lane_freq[64:128], kind[64:128] = freq[:64], 1
    lane_freq[128:160], kind[128:160] = freq[64:], 0
    lane_freq[192:224], kind[192:224] = freq[64:], 1
    angle = turn * (lane_freq[:, None] * cells[None, :] % N)
    cos, sin = np.cos(angle), np.sin(angle)
    re, im = (kind == 0)[:, None], (kind == 1)[:, None]
    to_re = re * cos - im * sin
    to_im = re * sin + im * cos
    norm = 1.0 / float(N) ** 3
    from_re = (re * cos - im * sin).T * norm
    from_im = (re * sin + im * cos).T * norm
    angle = turn * (plane[:, None] * paired[None, :] % N)
    middle_back = np.concatenate([np.cos(angle), np.sin(angle)], 0)
    angle = turn * (freq[:, None] * plane[None, :] % N)
    first_back = np.concatenate([np.cos(angle), np.sin(angle)], 0)
    tables = (first, middle, to_re, to_im, from_re, from_im, middle_back, first_back)
    return [np.stack(split(table)) for table in tables]


def halves(x):
    hi = x.astype(BF16)
    return hi, (x - hi.astype(F32)).astype(BF16)


def dot(a, b):
    return jnp.dot(a, b, preferred_element_type=F32)


def dot_left(table, hi, lo):
    return dot(table[0], hi) + dot(table[1], hi) + dot(table[0], lo)


def dot_right(hi, lo, table):
    return dot(hi, table[0]) + dot(lo, table[0]) + dot(hi, table[1])


def groups(x):
    return [x[:, 128 * g : 128 * g + 128] for g in range(x.shape[1] // 128)]


def combine(both, sign):
    rows = both.shape[0] // 2
    lane = lax.broadcasted_iota(jnp.int32, (rows, 128), 1)
    factor = jnp.where(lane < 64, -sign, sign).astype(F32)
    parts = [
        c + factor * pltpu.roll(s, 64, 1)
        for c, s in zip(groups(both[:rows]), groups(both[rows:]))
    ]
    return jnp.concatenate(parts, 1)


def kernel(
    index_hbm,
    coef_hbm,
    pot_hbm,
    first_hbm,
    middle_hbm,
    to_re_hbm,
    to_im_hbm,
    from_re_hbm,
    from_im_hbm,
    middle_back_hbm,
    first_back_hbm,
    sub_ref,
    res_ref,
    index_ref,
    coef_ref,
    pot_flat,
    first,
    middle,
    to_re,
    to_im,
    from_re,
    from_im,
    middle_back,
    first_back,
    load_sem,
    pot_rows,
    pot_ref,
    field_ref,
    row_key,
    col_key,
    coef_hi,
    coef_lo,
    acc,
    send1,
    recv1,
    send2,
    recv2,
    trash,
    all_coef,
    applied,
    part,
    parts_in,
    send_sem,
    recv_sem,
    band_send,
    band_recv,
    own_sem,
):
    sources = (
        (index_hbm, index_ref),
        (coef_hbm, coef_ref),
        (first_hbm, first),
        (middle_hbm, middle),
        (to_re_hbm, to_re),
        (to_im_hbm, to_im),
        (pot_hbm, pot_flat),
        (from_re_hbm, from_re),
        (from_im_hbm, from_im),
        (middle_back_hbm, middle_back),
        (first_back_hbm, first_back),
    )
    loads = [
        pltpu.make_async_copy(src, dst, load_sem.at[k]) for k, (src, dst) in enumerate(sources)
    ]
    for load in loads:
        load.start()

    me = lax.axis_index("grid")
    band = lax.axis_index("band")
    sibling = band + 1 - 2 * lax.rem(band, 2)
    across = lax.rem(band + 2, 4)
    opposite = lax.rem(sibling + 2, 4)

    barrier = pltpu.get_barrier_semaphore()

    def greet(i, carry):
        peer = lax.rem(me + i, PARTS)
        pl.semaphore_signal(barrier, inc=1, device_id={"grid": peer}, device_id_type=MESH)
        return carry

    lax.fori_loop(1, PARTS, greet, 0)
    pl.semaphore_signal(barrier, inc=1, device_id={"band": sibling}, device_id_type=MESH)
    pl.semaphore_signal(barrier, inc=1, device_id={"band": across}, device_id_type=MESH)

    loads[0].wait()
    loads[1].wait()
    cell = index_ref[...].astype(F32)
    line = jnp.floor((cell + 0.5) * (1.0 / N))
    gc = cell - N * line
    ga = jnp.floor((cell + 0.5) * (1.0 / (SLAB * N)))
    slab = line - SLAB * ga
    row_key[...] = slab * HALF + jnp.where(ga < HALF, ga, ga - HALF)
    col_key[...] = jnp.where(gc < HALF, gc, gc - HALF)
    coef = coef_ref[...]
    coef_hi[...] = coef.astype(BF16).astype(F32)
    coef_lo[...] = coef - coef.astype(BF16).astype(F32)
    acc[...] = jnp.zeros_like(acc)

    iota96 = lax.broadcasted_iota(jnp.int32, (HALF, 128), 0).astype(F32)
    iota96h = iota96.astype(BF16)
    one, zero = jnp.ones((), BF16), jnp.zeros((), BF16)
    zero32 = jnp.zeros((32, 128), BF16)

    def wide(x):
        return jnp.broadcast_to(x.astype(BF16), (HALF, 128))

    def row_hot(i):
        pieces = []
        for s in range(KS):
            key = row_key[pl.ds(i * KS + s, 1), :]
            pieces.append(
                jnp.concatenate(
                    [jnp.where(iota96h == wide(key - HALF * p), one, zero) for p in range(SLAB)], 0
                )
            )
        return jnp.concatenate(pieces, 1)

    def scatter_step(low, count):
        pad = [] if count == 64 else [zero32]
        iota = iota96h[:count]

        def step(i, carry):
            pieces = []
            for s in range(KS):
                row = pl.ds(i * KS + s, 1)
                mask = iota == jnp.broadcast_to((col_key[row, :] - low).astype(BF16), (count, 128))
                blocks = []
                for ref in (coef_hi, coef_lo):
                    for k in range(2):
                        value = jnp.broadcast_to(ref[k, row, :].astype(BF16), (count, 128))
                        blocks += [jnp.where(mask, value, zero)] + pad
                pieces.append(jnp.concatenate(blocks, 0))
            acc[low // 64] += lax.dot_general(
                row_hot(i),
                jnp.concatenate(pieces, 1),
                (((1,), (1,)), ((), ())),
                preferred_element_type=F32,
            )
            return carry

        return step

    steps = 128 // KS
    lax.fori_loop(0, steps // 2, scatter_step(0, 64), 0)
    pl.semaphore_wait(barrier, PARTS - 1 + 2)

    def band_copy(src, dst, slot, to):
        return pltpu.make_async_remote_copy(
            src_ref=src,
            dst_ref=dst,
            send_sem=band_send.at[slot],
            recv_sem=band_recv.at[slot],
            device_id={"band": to},
            device_id_type=MESH,
        )

    to_across = band_copy(coef_ref, all_coef.at[band], 0, across)
    to_sibling = band_copy(coef_ref, all_coef.at[band], 1, sibling)
    keep = pltpu.make_async_copy(coef_ref, all_coef.at[band], own_sem)
    to_across.start()
    to_sibling.start()
    keep.start()
    lax.fori_loop(steps // 2, steps, scatter_step(0, 64), 0)

    def exchange(src, dst, own, lanes, slot):
        def one_copy(i, carry):
            peer = lax.rem(me + i, PARTS)
            pltpu.make_async_remote_copy(
                src_ref=src.at[own, peer, lanes],
                dst_ref=dst.at[own, me, lanes],
                send_sem=send_sem.at[slot],
                recv_sem=recv_sem.at[slot],
                device_id={"grid": peer},
                device_id_type=MESH,
            ).start()
            return carry

        lax.fori_loop(1, PARTS, one_copy, 0)
        pltpu.make_async_copy(
            src.at[own, me, lanes], dst.at[own, me, lanes], recv_sem.at[slot]
        ).start()
        pltpu.make_async_copy(
            src.at[own, me, lanes], trash.at[own, slot, lanes], send_sem.at[slot]
        ).start()

    def arrive(src, dst, lanes, slot):
        pltpu.make_async_copy(src.at[:, :, lanes], dst.at[:, :, lanes], recv_sem.at[slot]).wait()

    def sent(src, dst, lanes, slot):
        pltpu.make_async_copy(src.at[:, :, lanes], dst.at[:, :, lanes], send_sem.at[slot]).wait()

    lanes_a, lanes_b = pl.ds(0, LA), pl.ds(LA, LB)

    every = pl.ds(0, SLAB)

    def spectrum_a(offset):
        a = [acc[0, HALF * p : HALF * p + HALF, offset : offset + 128] for p in range(SLAB)]
        return jnp.concatenate(a, 1).astype(BF16)

    def spectrum_b(offset):
        b = [acc[1, HALF * p : HALF * p + HALF, offset : offset + 128] for p in range(SLAB)]
        return jnp.concatenate([b[0] + pltpu.roll(b[1], 32, 1), b[2]], 1).astype(BF16)

    loads[2].wait()
    out = combine(dot_left(first, spectrum_a(0), spectrum_a(128)), 1.0)
    for j in range(SLAB):
        send1[j, :, 0:LA] = out[PARTS * j : PARTS * j + PARTS]
    exchange(send1, recv1, every, lanes_a, 0)
    lax.fori_loop(0, steps, scatter_step(64, 32), 0)
    out = combine(dot_left(first, spectrum_b(0), spectrum_b(128)), 1.0)
    for j in range(SLAB):
        send1[j, :, LA:LANES] = out[PARTS * j : PARTS * j + PARTS]
    exchange(send1, recv1, every, lanes_b, 1)

    band_copy(coef_ref, all_coef.at[across], 0, across).wait_recv()
    onward = band_copy(all_coef.at[across], all_coef.at[across], 2, sibling)
    onward.start()

    for load in loads[3:]:
        load.wait()

    def pot_row(q, carry):
        both = pot_flat[:, pl.ds(pl.multiple_of(q * 384, 128), 384)]
        for j in range(SLAB):
            pot_rows[j, pl.ds(q, 1), :] = both[j : j + 1]
        return carry

    lax.fori_loop(0, HALF, pot_row, 0)
    for j in range(SLAB):
        pot_ref[j, 0:HALF] = pot_rows[j, :, 0:N]
        pot_ref[j, HALF:N] = pltpu.roll(pot_rows[j], N, 1)[:, 0:N]

    arrive(send1, recv1, lanes_a, 0)

    def middle_a(j, carry):
        x = recv1[j, :, 0:LA]
        x = jnp.concatenate([x[:, 0:128], x[:, 128:256], x[:, 256:384]], 0)
        hi, lo = halves(combine(dot_left(middle, *halves(x)), 1.0))
        field_ref[j, 0] = dot_right(hi, lo, to_re[:, 0:128])
        field_ref[j, 1] = dot_right(hi, lo, to_im[:, 0:128])
        return carry

    lax.fori_loop(0, SLAB, middle_a, 0)
    arrive(send1, recv1, lanes_b, 1)

    def middle_b(j, carry):
        x = recv1[j, :, LA:LANES]
        x = jnp.concatenate([x[:, 0:128], pltpu.roll(x[:, 0:128], 96, 1), x[:, 128:256]], 0)
        hi, lo = halves(combine(dot_left(middle, *halves(x)), 1.0))
        pot = pot_ref[j]
        field_re = (field_ref[j, 0] + dot_right(hi, lo, to_re[:, 128:256])) * pot
        field_im = (field_ref[j, 1] + dot_right(hi, lo, to_im[:, 128:256])) * pot
        x = dot_right(*halves(field_re), from_re) + dot_right(*halves(field_im), from_im)
        x = combine(dot_left(middle_back, *halves(x)), -1.0)
        for p in range(SLAB):
            send2[j, :, 128 * p : 128 * p + 128] = x[PARTS * p : PARTS * p + PARTS, 0:128]
        send2[j, :, 384:512] = x[0:64, 128:256] + pltpu.roll(x[64:128, 128:256], 32, 1)
        send2[j, :, 512:640] = x[128:192, 128:256]
        exchange(send2, recv2, pl.ds(j, 1), lanes_a, 2)
        return carry

    lax.fori_loop(0, SLAB, middle_b, 0)
    exchange(send2, recv2, every, lanes_b, 3)

    def gather(low, count):
        def rows_of(x):
            if low == 0:
                return [x[:, 0:128], x[:, 128:256], x[:, 256:384]]
            return [x[:, 0:128], pltpu.roll(x[:, 0:128], 96, 1), x[:, 128:256]]

        x = recv2[:, :, 0:LA] if low == 0 else recv2[:, :, LA:LANES]
        x = combine(dot_left(first_back, *halves(x.reshape(N, x.shape[-1]))), -1.0)
        x = jnp.concatenate(rows_of(x), 0).T
        hi, lo = halves(jnp.concatenate([x[0:count], x[64 : 64 + count]], 0))
        table = jnp.concatenate([hi, lo], 0)
        iota = iota96[:count]

        def step(i, carry):
            found = dot(table, row_hot(i))
            found = found[: 2 * count] + found[2 * count :]
            for s in range(KS):
                row = pl.ds(i * KS + s, 1)
                mask = iota == jnp.broadcast_to(col_key[row, :] - low, (count, 128))
                here = found[:, 128 * s : 128 * s + 128]
                for k in range(2):
                    kept = jnp.where(mask, here[count * k : count * k + count], 0.0)
                    kept = kept.reshape(count // 8, 8, 128).sum(0).sum(0, keepdims=True)
                    applied[k, row, :] = kept if low == 0 else applied[k, row, :] + kept
            return carry

        lax.fori_loop(0, steps, step, 0)

    arrive(send2, recv2, lanes_a, 2)
    gather(0, 64)
    arrive(send2, recv2, lanes_b, 3)
    gather(64, 32)

    band_copy(coef_ref, all_coef.at[sibling], 1, sibling).wait_recv()
    band_copy(coef_ref, all_coef.at[opposite], 2, sibling).wait_recv()
    keep.wait()

    h_re, h_im = applied[0], applied[1]
    sums = []
    for i in range(4):
        c_re, c_im = all_coef[i, 0], all_coef[i, 1]
        sums.append((c_re * h_re + c_im * h_im, c_re * h_im - c_im * h_re))
    lanes = [s[0].sum(0, keepdims=True) for s in sums] + [s[1].sum(0, keepdims=True) for s in sums]
    total = jnp.concatenate(lanes, 0).sum(1, keepdims=True)
    eye = lax.broadcasted_iota(jnp.int32, (8, 128), 0) == lax.broadcasted_iota(
        jnp.int32, (8, 128), 1
    )
    line = jnp.where(eye, jnp.broadcast_to(total, (8, 128)), 0.0).sum(0, keepdims=True)
    part[...] = jnp.broadcast_to(line.reshape(1, 1, 128), part.shape)

    def share(i, carry):
        peer = lax.rem(me + i, PARTS)
        pltpu.make_async_remote_copy(
            src_ref=part.at[:, 0],
            dst_ref=parts_in.at[:, me],
            send_sem=send_sem.at[4],
            recv_sem=recv_sem.at[4],
            device_id={"grid": peer},
            device_id_type=MESH,
        ).start()
        return carry

    lax.fori_loop(1, PARTS, share, 0)
    pltpu.make_async_copy(part.at[:, 0], parts_in.at[:, me], recv_sem.at[4]).start()
    pltpu.make_async_copy(part.at[:, 0], trash.at[pl.ds(0, 1), 4, pl.ds(0, 128)], send_sem.at[4]).start()
    pltpu.make_async_copy(part, parts_in, recv_sem.at[4]).wait()

    line = parts_in[0].sum(0, keepdims=True) * (1.0 / (PARTS * 16384))
    sub_ref[0] = line[:, 0:4]
    sub_ref[1] = line[:, 4:8]
    r_re, r_im = h_re, h_im
    for i in range(4):
        s_re = jnp.broadcast_to(line[:, i : i + 1], (128, 128))
        s_im = jnp.broadcast_to(line[:, i + 4 : i + 5], (128, 128))
        c_re, c_im = all_coef[i, 0], all_coef[i, 1]
        r_re = r_re - (c_re * s_re - c_im * s_im)
        r_im = r_im - (c_re * s_im + c_im * s_re)
    res_ref[0] = r_re
    res_ref[1] = r_im

    sent(send1, recv1, lanes_a, 0)
    sent(send1, recv1, lanes_b, 1)
    sent(send2, recv2, lanes_a, 2)
    sent(send2, recv2, lanes_b, 3)
    pltpu.make_async_copy(part, parts_in, send_sem.at[4]).wait()
    to_across.wait_send()
    to_sibling.wait_send()
    onward.wait_send()


def local(coefficients, index_map, potential):
    tables = [jnp.asarray(t) for t in make_tables()]
    coef = coefficients.reshape(2, 128, 128)
    index = index_map.reshape(128, 128)
    inputs = (index, coef, potential, *tables)
    field = VMEM((SLAB, PARTS, LANES), F32)
    sub, res = pl.pallas_call(
        kernel,
        out_shape=(
            jax.ShapeDtypeStruct((2, 1, 4), F32),
            jax.ShapeDtypeStruct((2, 128, 128), F32),
        ),
        in_specs=[pl.BlockSpec(memory_space=pltpu.HBM)] * len(inputs),
        out_specs=[pl.BlockSpec(memory_space=VMEM)] * 2,
        scratch_shapes=[VMEM(x.shape, x.dtype) for x in inputs]
        + [
            pltpu.SemaphoreType.DMA((len(inputs),)),
            VMEM((SLAB, HALF, 384), F32),
            VMEM((SLAB, N, N), F32),
            VMEM((SLAB, 2, N, N), F32),
            VMEM((128, 128), F32),
            VMEM((128, 128), F32),
            VMEM((2, 128, 128), F32),
            VMEM((2, 128, 128), F32),
            VMEM((2, SLAB * HALF, 256), F32),
            field,
            field,
            field,
            field,
            VMEM((SLAB, 8, LANES), F32),
            VMEM((4, 2, 128, 128), F32),
            VMEM((2, 128, 128), F32),
            VMEM((1, PARTS, 128), F32),
            VMEM((1, PARTS, 128), F32),
            pltpu.SemaphoreType.DMA((5,)),
            pltpu.SemaphoreType.DMA((5,)),
            pltpu.SemaphoreType.DMA((3,)),
            pltpu.SemaphoreType.DMA((3,)),
            pltpu.SemaphoreType.DMA,
        ],
        compiler_params=pltpu.CompilerParams(
            collective_id=0, has_side_effects=True, vmem_limit_bytes=56 << 20
        ),
        name="apply_potential",
    )(*inputs)
    return sub.transpose(0, 2, 1), res.reshape(2, 1, 16384)


def solution(mesh):
    return jax.shard_map(
        local,
        mesh=mesh,
        in_specs=(P(None, "band", "grid"), P("grid"), P("grid", None)),
        out_specs=(P(None, None, "band"), P(None, "band", "grid")),
        check_vma=False,
    )
```

```python
import functools
import math

import jax
import jax.numpy as jnp
import ml_dtypes
import numpy as np
from jax import lax
from jax.experimental import pallas as pl
from jax.experimental.pallas import tpu as pltpu
from jax.sharding import PartitionSpec as P

N = 192
HALF = 96
PARTS = 64
SLAB = 3
KS = 32
LA, LB = 384, 256
LANES = LA + LB
F32, BF16 = jnp.float32, jnp.bfloat16
MESH = pl.DeviceIdType.MESH
VMEM = pltpu.VMEM


def split(table):
    hi = table.astype(np.float32).astype(ml_dtypes.bfloat16)
    lo = (table - hi.astype(np.float64)).astype(np.float32).astype(ml_dtypes.bfloat16)
    return hi, lo


def make_tables():
    turn = 2.0 * math.pi / N
    fold = np.arange(HALF)
    freq = np.where(fold < HALF // 2, fold, fold + HALF)
    plane = 3 * np.arange(PARTS)[None, :] + np.arange(SLAB)[:, None]
    plane = plane.reshape(-1)
    cells = np.arange(N)
    paired = np.concatenate([cells[0::2], cells[1::2]])
    angle = turn * (plane[:, None] * freq[None, :] % N)
    first = np.concatenate([np.cos(angle), np.sin(angle)], 0)
    angle = turn * (paired[:, None] * plane[None, :] % N)
    middle = np.concatenate([np.cos(angle), np.sin(angle)], 0)
    column = np.arange(HALF)
    column = np.where(column < 32, column, np.where(column < 64, column + 16, column))
    column[64:80] = np.arange(32, 48)
    col_freq = freq[column]
    lane_freq = np.zeros(256, np.int64)
    kind = np.full(256, -1)
    lane_freq[0:64], kind[0:64] = col_freq[:64], 0
    lane_freq[64:128], kind[64:128] = col_freq[:64], 1
    lane_freq[128:160], kind[128:160] = col_freq[64:], 0
    lane_freq[192:224], kind[192:224] = col_freq[64:], 1
    angle = turn * (lane_freq[:, None] * cells[None, :] % N)
    cos, sin = np.cos(angle), np.sin(angle)
    re, im = (kind == 0)[:, None], (kind == 1)[:, None]
    to_re = re * cos - im * sin
    to_im = re * sin + im * cos
    norm = 1.0 / float(N) ** 3
    from_re = (re * cos - im * sin).T * norm
    from_im = (re * sin + im * cos).T * norm
    angle = turn * (plane[:, None] * paired[None, :] % N)
    middle_back = np.concatenate([np.cos(angle), np.sin(angle)], 0)
    angle = turn * (freq[:, None] * plane[None, :] % N)
    first_back = np.concatenate([np.cos(angle), np.sin(angle)], 0)
    tables = (first, middle, to_re, to_im, from_re, from_im, middle_back, first_back)
    signed = np.where(fold < HALF // 2, fold, fold - HALF)
    moved = np.abs(signed) > 42
    home = np.where(moved, np.sign(signed) * (85 - np.abs(signed)), signed) % 85
    select = np.zeros((2, SLAB, HALF, 256), np.float32)
    for p in range(SLAB):
        for f in range(HALF):
            if f != HALF // 2:
                select[int(moved[f]), p, f, 85 * p + home[f]] = 1.0
    select = select.reshape(2, SLAB * HALF, 256).astype(ml_dtypes.bfloat16)
    row_fa = np.arange(256) % 85
    row_fa = np.where(row_fa < 43, row_fa, row_fa - 85)
    col_fc = signed[column]
    inside = row_fa[None, :] ** 2 + col_fc[:, None] ** 2 < (N // 4) ** 2
    return [np.stack(split(table)) for table in tables] + [select, inside.astype(np.float32)]


def halves(x):
    hi = x.astype(BF16)
    return hi, (x - hi.astype(F32)).astype(BF16)


def dot(a, b):
    return jnp.dot(a, b, preferred_element_type=F32)


def dot_left(table, hi, lo):
    return dot(table[0], hi) + dot(table[1], hi) + dot(table[0], lo)


def dot_right(hi, lo, table):
    return dot(hi, table[0]) + dot(lo, table[0]) + dot(hi, table[1])


def groups(x):
    return [x[:, 128 * g : 128 * g + 128] for g in range(x.shape[1] // 128)]


def combine(both, sign):
    rows = both.shape[0] // 2
    lane = lax.broadcasted_iota(jnp.int32, (rows, 128), 1)
    factor = jnp.where(lane < 64, -sign, sign).astype(F32)
    parts = [
        c + factor * pltpu.roll(s, 64, 1)
        for c, s in zip(groups(both[:rows]), groups(both[rows:]))
    ]
    return jnp.concatenate(parts, 1)


def kernel(
    index_hbm,
    coef_hbm,
    pot_hbm,
    first_hbm,
    middle_hbm,
    to_re_hbm,
    to_im_hbm,
    from_re_hbm,
    from_im_hbm,
    middle_back_hbm,
    first_back_hbm,
    select_hbm,
    inside_hbm,
    sub_ref,
    res_ref,
    index_ref,
    coef_ref,
    pot_flat,
    first,
    middle,
    to_re,
    to_im,
    from_re,
    from_im,
    middle_back,
    first_back,
    select,
    inside,
    load_sem,
    pot_rows,
    pot_ref,
    field_ref,
    row_key,
    col_key,
    row_home,
    col_home,
    coef_hi,
    coef_lo,
    acc,
    send1,
    recv1,
    send2,
    recv2,
    trash,
    all_coef,
    applied,
    part,
    parts_in,
    send_sem,
    recv_sem,
    band_send,
    band_recv,
    own_sem,
):
    sources = (
        (index_hbm, index_ref),
        (coef_hbm, coef_ref),
        (first_hbm, first),
        (middle_hbm, middle),
        (to_re_hbm, to_re),
        (to_im_hbm, to_im),
        (pot_hbm, pot_flat),
        (from_re_hbm, from_re),
        (from_im_hbm, from_im),
        (middle_back_hbm, middle_back),
        (first_back_hbm, first_back),
        (select_hbm, select),
        (inside_hbm, inside),
    )
    loads = [
        pltpu.make_async_copy(src, dst, load_sem.at[k]) for k, (src, dst) in enumerate(sources)
    ]
    for load in loads:
        load.start()

    me = lax.axis_index("grid")
    band = lax.axis_index("band")
    sibling = band + 1 - 2 * lax.rem(band, 2)
    across = lax.rem(band + 2, 4)
    opposite = lax.rem(sibling + 2, 4)

    barrier = pltpu.get_barrier_semaphore()

    def greet(i):
        pl.semaphore_signal(
            barrier,
            inc=1,
            device_id={
                "grid": lax.rem(me + i, PARTS),
                "band": jnp.where(i == 0, sibling, band),
            },
            device_id_type=MESH,
        )

    pl.semaphore_signal(barrier, inc=1, device_id={"band": across}, device_id_type=MESH)

    loads[0].wait()
    loads[1].wait()
    cell = index_ref[...].astype(F32)
    line = jnp.floor((cell + 0.5) * (1.0 / N))
    gc = cell - N * line
    ga = jnp.floor((cell + 0.5) * (1.0 / (SLAB * N)))
    slab = line - SLAB * ga
    row_key[...] = slab * HALF + jnp.where(ga < HALF, ga, ga - HALF)
    fold = jnp.where(gc < HALF, gc, gc - HALF)
    col = jnp.where(fold < 32, fold, jnp.where(fold < 80, fold - 16, fold))
    col = jnp.where(jnp.logical_and(fold >= 32, fold < 48), fold + 32, col)
    col_key[...] = col
    fa = jnp.where(ga < HALF, ga, ga - N)
    moved = jnp.abs(fa) > 42
    home = jnp.where(moved, jnp.where(fa > 0, 85 - fa, -85 - fa), fa)
    row_home[...] = slab * 85 + jnp.where(home < 0, home + 85, home)
    turned = jnp.where(
        col < 64,
        jnp.where(col < 32, col + 32, col - 32),
        jnp.where(col < 80, col + 16, col - 16),
    )
    col_home[...] = jnp.where(moved, turned, col)
    coef = coef_ref[...]
    coef_hi[...] = coef.astype(BF16).astype(F32)
    coef_lo[...] = coef - coef.astype(BF16).astype(F32)
    acc[...] = jnp.zeros_like(acc)

    iota96 = lax.broadcasted_iota(jnp.int32, (HALF, 128), 0).astype(F32)
    iota96h = iota96.astype(BF16)
    one, zero = jnp.ones((), BF16), jnp.zeros((), BF16)
    zero32 = jnp.zeros((32, 128), BF16)

    def wide(x):
        return jnp.broadcast_to(x.astype(BF16), (HALF, 128))

    def row_hot(i):
        pieces = []
        for s in range(KS):
            key = row_key[pl.ds(i * KS + s, 1), :]
            pieces.append(
                jnp.concatenate(
                    [jnp.where(iota96h == wide(key - HALF * p), one, zero) for p in range(SLAB)], 0
                )
            )
        return jnp.concatenate(pieces, 1)

    iota256h = lax.broadcasted_iota(jnp.int32, (256, 128), 0).astype(F32).astype(BF16)

    def home_hot(i):
        pieces = []
        for s in range(KS):
            key = row_home[pl.ds(i * KS + s, 1), :].astype(BF16)
            pieces.append(jnp.where(iota256h == jnp.broadcast_to(key, (256, 128)), one, zero))
        return jnp.concatenate(pieces, 1)

    def scatter_step(low, count):
        pad = [] if count == 64 else [zero32]
        iota = iota96h[:count]

        def step(i, carry):
            pieces = []
            for s in range(KS):
                row = pl.ds(i * KS + s, 1)
                mask = iota == jnp.broadcast_to((col_key[row, :] - low).astype(BF16), (count, 128))
                blocks = []
                for ref in (coef_hi, coef_lo):
                    for k in range(2):
                        value = jnp.broadcast_to(ref[k, row, :].astype(BF16), (count, 128))
                        blocks += [jnp.where(mask, value, zero)] + pad
                pieces.append(jnp.concatenate(blocks, 0))
            acc[low // 64] += lax.dot_general(
                row_hot(i),
                jnp.concatenate(pieces, 1),
                (((1,), (1,)), ((), ())),
                preferred_element_type=F32,
            )
            return carry

        return step

    steps = 128 // KS
    early = scatter_step(0, 64)

    def early_step(i, carry):
        for k in range(2 * PARTS // steps):
            greet(i * (2 * PARTS // steps) + k)
        return early(i, carry)

    lax.fori_loop(0, steps // 2, early_step, 0)
    pl.semaphore_wait(barrier, PARTS - 1 + 2)

    def band_copy(src, dst, slot, to):
        return pltpu.make_async_remote_copy(
            src_ref=src,
            dst_ref=dst,
            send_sem=band_send.at[slot],
            recv_sem=band_recv.at[slot],
            device_id={"band": to},
            device_id_type=MESH,
        )

    to_across = band_copy(coef_ref, all_coef.at[band], 0, across)
    to_sibling = band_copy(coef_ref, all_coef.at[band], 1, sibling)
    keep = pltpu.make_async_copy(coef_ref, all_coef.at[band], own_sem)
    to_across.start()
    to_sibling.start()
    keep.start()
    lax.fori_loop(steps // 2, steps, scatter_step(0, 64), 0)

    def exchange(src, dst, own, lanes, slot):
        def one_copy(i, carry):
            peer = lax.rem(me + i, PARTS)
            pltpu.make_async_remote_copy(
                src_ref=src.at[own, peer, lanes],
                dst_ref=dst.at[own, me, lanes],
                send_sem=send_sem.at[slot],
                recv_sem=recv_sem.at[slot],
                device_id={"grid": peer},
                device_id_type=MESH,
            ).start()
            return carry

        lax.fori_loop(1, PARTS, one_copy, 0)
        pltpu.make_async_copy(
            src.at[own, me, lanes], dst.at[own, me, lanes], recv_sem.at[slot]
        ).start()
        pltpu.make_async_copy(
            src.at[own, me, lanes], trash.at[own, slot, lanes], send_sem.at[slot]
        ).start()

    def arrive(src, dst, lanes, slot):
        pltpu.make_async_copy(src.at[:, :, lanes], dst.at[:, :, lanes], recv_sem.at[slot]).wait()

    def sent(src, dst, lanes, slot):
        pltpu.make_async_copy(src.at[:, :, lanes], dst.at[:, :, lanes], send_sem.at[slot]).wait()

    lanes_a, lanes_b = pl.ds(0, LA), pl.ds(LA, LB)

    every = pl.ds(0, SLAB)

    def spectrum_a(offset):
        a = [acc[0, HALF * p : HALF * p + HALF, offset : offset + 128] for p in range(SLAB)]
        return jnp.concatenate(a, 1).astype(BF16)

    def spectrum_b(offset):
        b = [acc[1, HALF * p : HALF * p + HALF, offset : offset + 128] for p in range(SLAB)]
        return jnp.concatenate([b[0] + pltpu.roll(b[1], 32, 1), b[2]], 1).astype(BF16)

    loads[2].wait()
    out = combine(dot_left(first, spectrum_a(0), spectrum_a(128)), 1.0)
    for j in range(SLAB):
        send1[j, :, 0:LA] = out[PARTS * j : PARTS * j + PARTS]
    exchange(send1, recv1, every, lanes_a, 0)
    lax.fori_loop(0, steps, scatter_step(64, 32), 0)
    out = combine(dot_left(first, spectrum_b(0), spectrum_b(128)), 1.0)
    for j in range(SLAB):
        send1[j, :, LA:LANES] = out[PARTS * j : PARTS * j + PARTS]
    exchange(send1, recv1, every, lanes_b, 1)

    band_copy(coef_ref, all_coef.at[across], 0, across).wait_recv()
    onward = band_copy(all_coef.at[across], all_coef.at[across], 2, sibling)
    onward.start()

    for load in loads[3:]:
        load.wait()

    def pot_row(q, carry):
        both = pot_flat[:, pl.ds(pl.multiple_of(q * 384, 128), 384)]
        for j in range(SLAB):
            pot_rows[j, pl.ds(q, 1), :] = both[j : j + 1]
        return carry

    lax.fori_loop(0, HALF, pot_row, 0)
    for j in range(SLAB):
        pot_ref[j, 0:HALF] = pot_rows[j, :, 0:N]
        pot_ref[j, HALF:N] = pltpu.roll(pot_rows[j], N, 1)[:, 0:N]

    arrive(send1, recv1, lanes_a, 0)

    def middle_a(j, carry):
        x = recv1[j, :, 0:LA]
        x = jnp.concatenate([x[:, 0:128], x[:, 128:256], x[:, 256:384]], 0)
        hi, lo = halves(combine(dot_left(middle, *halves(x)), 1.0))
        field_ref[j, 0] = dot_right(hi, lo, to_re[:, 0:128])
        field_ref[j, 1] = dot_right(hi, lo, to_im[:, 0:128])
        return carry

    lax.fori_loop(0, SLAB, middle_a, 0)
    arrive(send1, recv1, lanes_b, 1)

    def middle_b(j, carry):
        x = recv1[j, :, LA:LANES]
        x = jnp.concatenate([x[:, 0:128], pltpu.roll(x[:, 0:128], 96, 1), x[:, 128:256]], 0)
        hi, lo = halves(combine(dot_left(middle, *halves(x)), 1.0))
        pot = pot_ref[j]
        field_re = (field_ref[j, 0] + dot_right(hi, lo, to_re[:, 128:256])) * pot
        field_im = (field_ref[j, 1] + dot_right(hi, lo, to_im[:, 128:256])) * pot
        x = dot_right(*halves(field_re), from_re) + dot_right(*halves(field_im), from_im)
        x = combine(dot_left(middle_back, *halves(x)), -1.0)
        for p in range(SLAB):
            send2[j, :, 128 * p : 128 * p + 128] = x[PARTS * p : PARTS * p + PARTS, 0:128]
        send2[j, :, 384:512] = x[0:64, 128:256] + pltpu.roll(x[64:128, 128:256], 32, 1)
        send2[j, :, 512:640] = x[128:192, 128:256]
        exchange(send2, recv2, pl.ds(j, 1), lanes_a, 2)
        return carry

    lax.fori_loop(0, SLAB, middle_b, 0)
    exchange(send2, recv2, every, lanes_b, 3)

    def gather(low, count):
        def rows_of(x):
            if low == 0:
                return [x[:, 0:128], x[:, 128:256], x[:, 256:384]]
            return [x[:, 0:128], pltpu.roll(x[:, 0:128], 96, 1), x[:, 128:256]]

        x = recv2[:, :, 0:LA] if low == 0 else recv2[:, :, LA:LANES]
        x = combine(dot_left(first_back, *halves(x.reshape(N, x.shape[-1]))), -1.0)
        x = jnp.concatenate(rows_of(x), 0).T
        hi, lo = halves(jnp.concatenate([x[0:count], x[64 : 64 + count]], 0))
        table = jnp.concatenate([hi, lo], 0)
        turned = []
        for k in range(4):
            block = table[count * k : count * k + count]
            turned += [block[count // 2 :], block[: count // 2]]
        keep_own = inside[low : low + count, :]
        table = jnp.where(
            jnp.concatenate([keep_own] * 4, 0) > 0.5,
            dot(table, select[0]),
            dot(jnp.concatenate(turned, 0), select[1]),
        ).astype(BF16)
        iota = iota96[:count]

        def step(i, carry):
            found = dot(table, home_hot(i))
            found = found[: 2 * count] + found[2 * count :]
            for s in range(KS):
                row = pl.ds(i * KS + s, 1)
                mask = iota == jnp.broadcast_to(col_home[row, :] - low, (count, 128))
                here = found[:, 128 * s : 128 * s + 128]
                for k in range(2):
                    kept = jnp.where(mask, here[count * k : count * k + count], 0.0)
                    kept = kept.reshape(count // 8, 8, 128).sum(0).sum(0, keepdims=True)
                    applied[k, row, :] = kept if low == 0 else applied[k, row, :] + kept
            return carry

        lax.fori_loop(0, steps, step, 0)

    arrive(send2, recv2, lanes_a, 2)
    gather(0, 64)
    arrive(send2, recv2, lanes_b, 3)
    gather(64, 32)

    band_copy(coef_ref, all_coef.at[sibling], 1, sibling).wait_recv()
    band_copy(coef_ref, all_coef.at[opposite], 2, sibling).wait_recv()
    keep.wait()

    h_re, h_im = applied[0], applied[1]
    sums = []
    for i in range(4):
        c_re, c_im = all_coef[i, 0], all_coef[i, 1]
        sums.append((c_re * h_re + c_im * h_im, c_re * h_im - c_im * h_re))
    lanes = [s[0].sum(0, keepdims=True) for s in sums] + [s[1].sum(0, keepdims=True) for s in sums]
    total = jnp.concatenate(lanes, 0).sum(1, keepdims=True)
    eye = lax.broadcasted_iota(jnp.int32, (8, 128), 0) == lax.broadcasted_iota(
        jnp.int32, (8, 128), 1
    )
    line = jnp.where(eye, jnp.broadcast_to(total, (8, 128)), 0.0).sum(0, keepdims=True)
    part[...] = jnp.broadcast_to(line.reshape(1, 1, 128), part.shape)

    def share(i, carry):
        peer = lax.rem(me + i, PARTS)
        pltpu.make_async_remote_copy(
            src_ref=part.at[:, 0],
            dst_ref=parts_in.at[:, me],
            send_sem=send_sem.at[4],
            recv_sem=recv_sem.at[4],
            device_id={"grid": peer},
            device_id_type=MESH,
        ).start()
        return carry

    lax.fori_loop(1, PARTS, share, 0)
    pltpu.make_async_copy(part.at[:, 0], parts_in.at[:, me], recv_sem.at[4]).start()
    pltpu.make_async_copy(part.at[:, 0], trash.at[pl.ds(0, 1), 4, pl.ds(0, 128)], send_sem.at[4]).start()
    pltpu.make_async_copy(part, parts_in, recv_sem.at[4]).wait()

    line = parts_in[0].sum(0, keepdims=True) * (1.0 / (PARTS * 16384))
    sub_ref[0] = line[:, 0:4]
    sub_ref[1] = line[:, 4:8]
    r_re, r_im = h_re, h_im
    for i in range(4):
        s_re = jnp.broadcast_to(line[:, i : i + 1], (128, 128))
        s_im = jnp.broadcast_to(line[:, i + 4 : i + 5], (128, 128))
        c_re, c_im = all_coef[i, 0], all_coef[i, 1]
        r_re = r_re - (c_re * s_re - c_im * s_im)
        r_im = r_im - (c_re * s_im + c_im * s_re)
    res_ref[0] = r_re
    res_ref[1] = r_im

    sent(send1, recv1, lanes_a, 0)
    sent(send1, recv1, lanes_b, 1)
    sent(send2, recv2, lanes_a, 2)
    sent(send2, recv2, lanes_b, 3)
    pltpu.make_async_copy(part, parts_in, send_sem.at[4]).wait()
    to_across.wait_send()
    to_sibling.wait_send()
    onward.wait_send()


def local(coefficients, index_map, potential):
    tables = [jnp.asarray(t) for t in make_tables()]
    coef = coefficients.reshape(2, 128, 128)
    index = index_map.reshape(128, 128)
    inputs = (index, coef, potential, *tables)
    field = VMEM((SLAB, PARTS, LANES), F32)
    sub, res = pl.pallas_call(
        kernel,
        out_shape=(
            jax.ShapeDtypeStruct((2, 1, 4), F32),
            jax.ShapeDtypeStruct((2, 128, 128), F32),
        ),
        in_specs=[pl.BlockSpec(memory_space=pltpu.HBM)] * len(inputs),
        out_specs=[pl.BlockSpec(memory_space=VMEM)] * 2,
        scratch_shapes=[VMEM(x.shape, x.dtype) for x in inputs]
        + [
            pltpu.SemaphoreType.DMA((len(inputs),)),
            VMEM((SLAB, HALF, 384), F32),
            VMEM((SLAB, N, N), F32),
            VMEM((SLAB, 2, N, N), F32),
            VMEM((128, 128), F32),
            VMEM((128, 128), F32),
            VMEM((128, 128), F32),
            VMEM((128, 128), F32),
            VMEM((2, 128, 128), F32),
            VMEM((2, 128, 128), F32),
            VMEM((2, SLAB * HALF, 256), F32),
            field,
            field,
            field,
            field,
            VMEM((SLAB, 8, LANES), F32),
            VMEM((4, 2, 128, 128), F32),
            VMEM((2, 128, 128), F32),
            VMEM((1, PARTS, 128), F32),
            VMEM((1, PARTS, 128), F32),
            pltpu.SemaphoreType.DMA((5,)),
            pltpu.SemaphoreType.DMA((5,)),
            pltpu.SemaphoreType.DMA((3,)),
            pltpu.SemaphoreType.DMA((3,)),
            pltpu.SemaphoreType.DMA,
        ],
        compiler_params=pltpu.CompilerParams(
            collective_id=0, has_side_effects=True, vmem_limit_bytes=56 << 20
        ),
        name="apply_potential",
    )(*inputs)
    return sub.transpose(0, 2, 1), res.reshape(2, 1, 16384)


def solution(mesh):
    return jax.shard_map(
        local,
        mesh=mesh,
        in_specs=(P(None, "band", "grid"), P("grid"), P("grid", None)),
        out_specs=(P(None, None, "band"), P(None, "band", "grid")),
        check_vma=False,
    )
```

```python
import functools
import math

import jax
import jax.numpy as jnp
import ml_dtypes
import numpy as np
from jax import lax
from jax.experimental import pallas as pl
from jax.experimental.pallas import tpu as pltpu
from jax.sharding import PartitionSpec as P

N = 192
HALF = 96
PARTS = 64
SLAB = 3
KS = 64
LA, LB = 384, 256
LANES = LA + LB
F32, BF16 = jnp.float32, jnp.bfloat16
MESH = pl.DeviceIdType.MESH
VMEM = pltpu.VMEM


def split(table):
    hi = table.astype(np.float32).astype(ml_dtypes.bfloat16)
    lo = (table - hi.astype(np.float64)).astype(np.float32).astype(ml_dtypes.bfloat16)
    return hi, lo


def make_tables():
    turn = 2.0 * math.pi / N
    fold = np.arange(HALF)
    freq = np.where(fold < HALF // 2, fold, fold + HALF)
    plane = 3 * np.arange(PARTS)[None, :] + np.arange(SLAB)[:, None]
    plane = plane.reshape(-1)
    cells = np.arange(N)
    paired = np.concatenate([cells[0::2], cells[1::2]])
    angle = turn * (plane[:, None] * freq[None, :] % N)
    first = np.concatenate([np.cos(angle), np.sin(angle)], 0)
    angle = turn * (paired[:, None] * plane[None, :] % N)
    middle = np.concatenate([np.cos(angle), np.sin(angle)], 0)
    column = np.arange(HALF)
    column = np.where(column < 32, column, np.where(column < 64, column + 16, column))
    column[64:80] = np.arange(32, 48)
    col_freq = freq[column]
    lane_freq = np.zeros(256, np.int64)
    kind = np.full(256, -1)
    lane_freq[0:64], kind[0:64] = col_freq[:64], 0
    lane_freq[64:128], kind[64:128] = col_freq[:64], 1
    lane_freq[128:160], kind[128:160] = col_freq[64:], 0
    lane_freq[192:224], kind[192:224] = col_freq[64:], 1
    angle = turn * (lane_freq[:, None] * cells[None, :] % N)
    cos, sin = np.cos(angle), np.sin(angle)
    re, im = (kind == 0)[:, None], (kind == 1)[:, None]
    to_re = re * cos - im * sin
    to_im = re * sin + im * cos
    norm = 1.0 / float(N) ** 3
    from_re = (re * cos - im * sin).T * norm
    from_im = (re * sin + im * cos).T * norm
    angle = turn * (plane[:, None] * paired[None, :] % N)
    middle_back = np.concatenate([np.cos(angle), np.sin(angle)], 0)
    angle = turn * (freq[:, None] * plane[None, :] % N)
    first_back = np.concatenate([np.cos(angle), np.sin(angle)], 0)
    tables = (first, middle, to_re, to_im, from_re, from_im, middle_back, first_back)
    signed = np.where(fold < HALF // 2, fold, fold - HALF)
    moved = np.abs(signed) > 42
    home = np.where(moved, np.sign(signed) * (85 - np.abs(signed)), signed) % 85
    select = np.zeros((2, SLAB, HALF, 256), np.float32)
    for p in range(SLAB):
        for f in range(HALF):
            if f != HALF // 2:
                select[int(moved[f]), p, f, 85 * p + home[f]] = 1.0
    select = select.reshape(2, SLAB * HALF, 256).astype(ml_dtypes.bfloat16)
    row_fa = np.arange(256) % 85
    row_fa = np.where(row_fa < 43, row_fa, row_fa - 85)
    col_fc = signed[column]
    inside = row_fa[None, :] ** 2 + col_fc[:, None] ** 2 < (N // 4) ** 2
    return [np.stack(split(table)) for table in tables] + [select, inside.astype(np.float32)]


def halves(x):
    hi = x.astype(BF16)
    return hi, (x - hi.astype(F32)).astype(BF16)


def dot(a, b):
    return jnp.dot(a, b, preferred_element_type=F32)


def dot_left(table, hi, lo):
    return dot(table[0], hi) + dot(table[1], hi) + dot(table[0], lo)


def dot_right(hi, lo, table):
    return dot(hi, table[0]) + dot(lo, table[0]) + dot(hi, table[1])


def groups(x):
    return [x[:, 128 * g : 128 * g + 128] for g in range(x.shape[1] // 128)]


def combine(both, sign):
    rows = both.shape[0] // 2
    lane = lax.broadcasted_iota(jnp.int32, (rows, 128), 1)
    factor = jnp.where(lane < 64, -sign, sign).astype(F32)
    parts = [
        c + factor * pltpu.roll(s, 64, 1)
        for c, s in zip(groups(both[:rows]), groups(both[rows:]))
    ]
    return jnp.concatenate(parts, 1)


def kernel(
    index_hbm,
    coef_hbm,
    pot_hbm,
    first_hbm,
    middle_hbm,
    to_re_hbm,
    to_im_hbm,
    from_re_hbm,
    from_im_hbm,
    middle_back_hbm,
    first_back_hbm,
    select_hbm,
    inside_hbm,
    sub_ref,
    res_ref,
    index_ref,
    coef_ref,
    pot_flat,
    first,
    middle,
    to_re,
    to_im,
    from_re,
    from_im,
    middle_back,
    first_back,
    select,
    inside,
    load_sem,
    pot_rows,
    pot_ref,
    field_ref,
    row_key,
    col_key,
    row_home,
    col_home,
    coef_hi,
    coef_lo,
    acc,
    send1,
    recv1,
    send2,
    recv2,
    trash,
    last_plane,
    all_coef,
    applied,
    part,
    parts_in,
    send_sem,
    recv_sem,
    band_send,
    band_recv,
    own_sem,
):
    sources = (
        (index_hbm, index_ref),
        (coef_hbm, coef_ref),
        (first_hbm, first),
        (middle_hbm, middle),
        (to_re_hbm, to_re),
        (to_im_hbm, to_im),
        (pot_hbm, pot_flat),
        (from_re_hbm, from_re),
        (from_im_hbm, from_im),
        (middle_back_hbm, middle_back),
        (first_back_hbm, first_back),
        (select_hbm, select),
        (inside_hbm, inside),
    )
    loads = [
        pltpu.make_async_copy(src, dst, load_sem.at[k]) for k, (src, dst) in enumerate(sources)
    ]
    for load in loads:
        load.start()

    me = lax.axis_index("grid")
    band = lax.axis_index("band")
    sibling = band + 1 - 2 * lax.rem(band, 2)
    across = lax.rem(band + 2, 4)
    opposite = lax.rem(sibling + 2, 4)

    barrier = pltpu.get_barrier_semaphore()

    def greet(i):
        pl.semaphore_signal(
            barrier,
            inc=1,
            device_id={
                "grid": lax.rem(me + i, PARTS),
                "band": jnp.where(i == 0, sibling, band),
            },
            device_id_type=MESH,
        )

    pl.semaphore_signal(barrier, inc=1, device_id={"band": across}, device_id_type=MESH)

    loads[0].wait()
    loads[1].wait()
    cell = index_ref[...].astype(F32)
    line = jnp.floor((cell + 0.5) * (1.0 / N))
    gc = cell - N * line
    ga = jnp.floor((cell + 0.5) * (1.0 / (SLAB * N)))
    slab = line - SLAB * ga
    row_key[...] = slab * HALF + jnp.where(ga < HALF, ga, ga - HALF)
    fold = jnp.where(gc < HALF, gc, gc - HALF)
    col = jnp.where(fold < 32, fold, jnp.where(fold < 80, fold - 16, fold))
    col = jnp.where(jnp.logical_and(fold >= 32, fold < 48), fold + 32, col)
    col_key[...] = col
    fa = jnp.where(ga < HALF, ga, ga - N)
    moved = jnp.abs(fa) > 42
    home = jnp.where(moved, jnp.where(fa > 0, 85 - fa, -85 - fa), fa)
    row_home[...] = slab * 85 + jnp.where(home < 0, home + 85, home)
    turned = jnp.where(
        col < 64,
        jnp.where(col < 32, col + 32, col - 32),
        jnp.where(col < 80, col + 16, col - 16),
    )
    col_home[...] = jnp.where(moved, turned, col)
    coef = coef_ref[...]
    coef_hi[...] = coef.astype(BF16).astype(F32)
    coef_lo[...] = coef - coef.astype(BF16).astype(F32)
    acc[...] = jnp.zeros_like(acc)

    iota96 = lax.broadcasted_iota(jnp.int32, (HALF, 128), 0).astype(F32)
    iota96h = iota96.astype(BF16)
    one, zero = jnp.ones((), BF16), jnp.zeros((), BF16)
    zero32 = jnp.zeros((32, 128), BF16)

    def wide(x):
        return jnp.broadcast_to(x.astype(BF16), (HALF, 128))

    def row_hot(i):
        pieces = []
        for s in range(KS):
            key = row_key[pl.ds(i * KS + s, 1), :]
            pieces.append(
                jnp.concatenate(
                    [jnp.where(iota96h == wide(key - HALF * p), one, zero) for p in range(SLAB)], 0
                )
            )
        return jnp.concatenate(pieces, 1)

    iota256h = lax.broadcasted_iota(jnp.int32, (256, 128), 0).astype(F32).astype(BF16)

    def home_hot(i):
        pieces = []
        for s in range(KS):
            key = row_home[pl.ds(i * KS + s, 1), :].astype(BF16)
            pieces.append(jnp.where(iota256h == jnp.broadcast_to(key, (256, 128)), one, zero))
        return jnp.concatenate(pieces, 1)

    def scatter_step(low, count):
        pad = [] if count == 64 else [zero32]
        iota = iota96h[:count]

        def step(i, carry):
            pieces = []
            for s in range(KS):
                row = pl.ds(i * KS + s, 1)
                mask = iota == jnp.broadcast_to((col_key[row, :] - low).astype(BF16), (count, 128))
                blocks = []
                for ref in (coef_hi, coef_lo):
                    for k in range(2):
                        value = jnp.broadcast_to(ref[k, row, :].astype(BF16), (count, 128))
                        blocks += [jnp.where(mask, value, zero)] + pad
                pieces.append(jnp.concatenate(blocks, 0))
            acc[low // 64] += lax.dot_general(
                row_hot(i),
                jnp.concatenate(pieces, 1),
                (((1,), (1,)), ((), ())),
                preferred_element_type=F32,
            )
            return carry

        return step

    steps = 128 // KS
    early = scatter_step(0, 64)

    def early_step(i, carry):
        for k in range(2 * PARTS // steps):
            greet(i * (2 * PARTS // steps) + k)
        return early(i, carry)

    lax.fori_loop(0, steps // 2, early_step, 0)
    pl.semaphore_wait(barrier, PARTS - 1 + 2)

    def band_copy(src, dst, slot, to):
        return pltpu.make_async_remote_copy(
            src_ref=src,
            dst_ref=dst,
            send_sem=band_send.at[slot],
            recv_sem=band_recv.at[slot],
            device_id={"band": to},
            device_id_type=MESH,
        )

    def to_across(k):
        return band_copy(coef_ref.at[k], all_coef.at[band, k], k, across)

    def onward(k):
        return band_copy(all_coef.at[across, k], all_coef.at[across, k], 3 + k, sibling)

    to_sibling = band_copy(coef_ref, all_coef.at[band], 2, sibling)
    keep = pltpu.make_async_copy(coef_ref, all_coef.at[band], own_sem)
    to_across(0).start()
    to_sibling.start()
    keep.start()
    lax.fori_loop(steps // 2, steps, scatter_step(0, 64), 0)

    def exchange(src, dst, own, lanes, slot):
        def one_copy(i, carry):
            peer = lax.rem(me + i, PARTS)
            pltpu.make_async_remote_copy(
                src_ref=src.at[own, peer, lanes],
                dst_ref=dst.at[own, me, lanes],
                send_sem=send_sem.at[slot],
                recv_sem=recv_sem.at[slot],
                device_id={"grid": peer},
                device_id_type=MESH,
            ).start()
            return carry

        lax.fori_loop(1, PARTS, one_copy, 0)
        pltpu.make_async_copy(
            src.at[own, me, lanes], dst.at[own, me, lanes], recv_sem.at[slot]
        ).start()
        pltpu.make_async_copy(
            src.at[own, me, lanes], trash.at[own, slot, lanes], send_sem.at[slot]
        ).start()

    def arrive(src, dst, lanes, slot, own=pl.ds(0, SLAB)):
        pltpu.make_async_copy(
            src.at[own, :, lanes], dst.at[own, :, lanes], recv_sem.at[slot]
        ).wait()

    def sent(src, dst, lanes, slot, own=pl.ds(0, SLAB)):
        pltpu.make_async_copy(
            src.at[own, :, lanes], dst.at[own, :, lanes], send_sem.at[slot]
        ).wait()

    lanes_a, lanes_b, lanes_c = pl.ds(0, LA), pl.ds(LA, 128), pl.ds(LA + 128, 128)
    every, two = pl.ds(0, SLAB), pl.ds(0, 2)

    def spectrum_a(offset):
        a = [acc[0, HALF * p : HALF * p + HALF, offset : offset + 128] for p in range(SLAB)]
        return jnp.concatenate(a, 1).astype(BF16)

    def spectrum_b(offset):
        b = [acc[1, HALF * p : HALF * p + HALF, offset : offset + 128] for p in range(SLAB)]
        return jnp.concatenate([b[0] + pltpu.roll(b[1], 32, 1), b[2]], 1).astype(BF16)

    loads[2].wait()
    out = combine(dot_left(first, spectrum_a(0), spectrum_a(128)), 1.0)
    for j in range(SLAB):
        send1[j, :, 0:LA] = out[PARTS * j : PARTS * j + PARTS]
    exchange(send1, recv1, every, lanes_a, 0)
    lax.fori_loop(0, steps, scatter_step(64, 32), 0)
    out = combine(dot_left(first, spectrum_b(0), spectrum_b(128)), 1.0)
    for j in range(SLAB):
        send1[j, :, LA : LA + 128] = out[PARTS * j : PARTS * j + PARTS, 0:128]
    send1[0, :, 512:640] = out[0:64, 128:256] + pltpu.roll(out[64:128, 128:256], 32, 1)
    send1[1, :, 512:640] = out[128:192, 128:256]
    exchange(send1, recv1, every, lanes_b, 1)
    exchange(send1, recv1, two, lanes_c, 5)

    band_copy(coef_ref.at[0], all_coef.at[across, 0], 0, across).wait_recv()
    onward(0).start()

    for load in loads[3:]:
        load.wait()

    def pot_row(q, carry):
        both = pot_flat[:, pl.ds(pl.multiple_of(q * 384, 128), 384)]
        for j in range(SLAB):
            pot_rows[j, pl.ds(q, 1), :] = both[j : j + 1]
        return carry

    lax.fori_loop(0, HALF, pot_row, 0)
    for j in range(SLAB):
        pot_ref[j, 0:HALF] = pot_rows[j, :, 0:N]
        pot_ref[j, HALF:N] = pltpu.roll(pot_rows[j], N, 1)[:, 0:N]

    arrive(send1, recv1, lanes_a, 0)

    def middle_a(j, carry):
        x = recv1[j, :, 0:LA]
        x = jnp.concatenate([x[:, 0:128], x[:, 128:256], x[:, 256:384]], 0)
        hi, lo = halves(combine(dot_left(middle, *halves(x)), 1.0))
        field_ref[j, 0] = dot_right(hi, lo, to_re[:, 0:128])
        field_ref[j, 1] = dot_right(hi, lo, to_im[:, 0:128])
        return carry

    lax.fori_loop(0, SLAB, middle_a, 0)
    arrive(send1, recv1, lanes_b, 1)
    arrive(send1, recv1, lanes_c, 5, two)

    def middle_b(j, carry):
        x = recv1[j, :, LA : LA + 128]
        y = recv1[j // 2, :, 512:640]
        y = jnp.where(j == 1, pltpu.roll(y, 96, 1), y)
        x = jnp.concatenate([x, pltpu.roll(x, 96, 1), y], 0)
        hi, lo = halves(combine(dot_left(middle, *halves(x)), 1.0))
        pot = pot_ref[j]
        field_re = (field_ref[j, 0] + dot_right(hi, lo, to_re[:, 128:256])) * pot
        field_im = (field_ref[j, 1] + dot_right(hi, lo, to_im[:, 128:256])) * pot
        x = dot_right(*halves(field_re), from_re) + dot_right(*halves(field_im), from_im)
        x = combine(dot_left(middle_back, *halves(x)), -1.0)
        for p in range(SLAB):
            send2[j, :, 128 * p : 128 * p + 128] = x[PARTS * p : PARTS * p + PARTS, 0:128]
        send2[j, :, 384:512] = x[0:64, 128:256] + pltpu.roll(x[64:128, 128:256], 32, 1)
        last_plane[j] = x[128:192, 128:256]
        exchange(send2, recv2, pl.ds(j, 1), lanes_a, 2)
        return carry

    to_across(1).start()
    lax.fori_loop(0, SLAB, middle_b, 0)
    exchange(send2, recv2, every, lanes_b, 3)
    send2[0, :, 512:640] = last_plane[0] + pltpu.roll(last_plane[1], 32, 1)
    send2[1, :, 512:640] = last_plane[2]
    exchange(send2, recv2, two, lanes_c, 6)

    def gather(low, count):
        def rows_of(x):
            if low == 0:
                return [x[:, 0:128], x[:, 128:256], x[:, 256:384]]
            return [x[:, 0:128], pltpu.roll(x[:, 0:128], 96, 1), x[:, 128:256]]

        if low == 0:
            x = recv2[:, :, 0:LA].reshape(N, LA)
        else:
            y = recv2[0, :, 512:640]
            y = jnp.concatenate([y, pltpu.roll(y, 96, 1), recv2[1, :, 512:640]], 0)
            x = jnp.concatenate([recv2[:, :, LA : LA + 128].reshape(N, 128), y], 1)
        x = combine(dot_left(first_back, *halves(x)), -1.0)
        x = jnp.concatenate(rows_of(x), 0).T
        hi, lo = halves(jnp.concatenate([x[0:count], x[64 : 64 + count]], 0))
        table = jnp.concatenate([hi, lo], 0)
        turned = []
        for k in range(4):
            block = table[count * k : count * k + count]
            turned += [block[count // 2 :], block[: count // 2]]
        keep_own = inside[low : low + count, :]
        table = jnp.where(
            jnp.concatenate([keep_own] * 4, 0) > 0.5,
            dot(table, select[0]),
            dot(jnp.concatenate(turned, 0), select[1]),
        ).astype(BF16)
        iota = iota96[:count]

        def step(i, carry):
            found = dot(table, home_hot(i))
            found = found[: 2 * count] + found[2 * count :]
            for s in range(KS):
                row = pl.ds(i * KS + s, 1)
                mask = iota == jnp.broadcast_to(col_home[row, :] - low, (count, 128))
                here = found[:, 128 * s : 128 * s + 128]
                for k in range(2):
                    kept = jnp.where(mask, here[count * k : count * k + count], 0.0)
                    kept = kept.reshape(count // 8, 8, 128).sum(0).sum(0, keepdims=True)
                    applied[k, row, :] = kept if low == 0 else applied[k, row, :] + kept
            return carry

        lax.fori_loop(0, steps, step, 0)

    band_copy(coef_ref.at[1], all_coef.at[across, 1], 1, across).wait_recv()
    onward(1).start()
    arrive(send2, recv2, lanes_a, 2)
    gather(0, 64)
    arrive(send2, recv2, lanes_b, 3)
    arrive(send2, recv2, lanes_c, 6, two)
    gather(64, 32)

    band_copy(coef_ref, all_coef.at[sibling], 2, sibling).wait_recv()
    for k in range(2):
        band_copy(coef_ref.at[k], all_coef.at[opposite, k], 3 + k, sibling).wait_recv()
    keep.wait()

    h_re, h_im = applied[0], applied[1]
    sums = []
    for i in range(4):
        c_re, c_im = all_coef[i, 0], all_coef[i, 1]
        sums.append((c_re * h_re + c_im * h_im, c_re * h_im - c_im * h_re))
    lanes = [s[0].sum(0, keepdims=True) for s in sums] + [s[1].sum(0, keepdims=True) for s in sums]
    total = jnp.concatenate(lanes, 0).sum(1, keepdims=True)
    eye = lax.broadcasted_iota(jnp.int32, (8, 128), 0) == lax.broadcasted_iota(
        jnp.int32, (8, 128), 1
    )
    line = jnp.where(eye, jnp.broadcast_to(total, (8, 128)), 0.0).sum(0, keepdims=True)
    part[...] = jnp.broadcast_to(line.reshape(1, 1, 128), part.shape)

    def share(i, carry):
        peer = lax.rem(me + i, PARTS)
        pltpu.make_async_remote_copy(
            src_ref=part.at[:, 0],
            dst_ref=parts_in.at[:, me],
            send_sem=send_sem.at[4],
            recv_sem=recv_sem.at[4],
            device_id={"grid": peer},
            device_id_type=MESH,
        ).start()
        return carry

    lax.fori_loop(1, PARTS, share, 0)
    pltpu.make_async_copy(part.at[:, 0], parts_in.at[:, me], recv_sem.at[4]).start()
    pltpu.make_async_copy(part.at[:, 0], trash.at[pl.ds(0, 1), 4, pl.ds(0, 128)], send_sem.at[4]).start()
    pltpu.make_async_copy(part, parts_in, recv_sem.at[4]).wait()

    line = parts_in[0].sum(0, keepdims=True) * (1.0 / (PARTS * 16384))
    sub_ref[0] = line[:, 0:4]
    sub_ref[1] = line[:, 4:8]
    r_re, r_im = h_re, h_im
    for i in range(4):
        s_re = jnp.broadcast_to(line[:, i : i + 1], (128, 128))
        s_im = jnp.broadcast_to(line[:, i + 4 : i + 5], (128, 128))
        c_re, c_im = all_coef[i, 0], all_coef[i, 1]
        r_re = r_re - (c_re * s_re - c_im * s_im)
        r_im = r_im - (c_re * s_im + c_im * s_re)
    res_ref[0] = r_re
    res_ref[1] = r_im

    sent(send1, recv1, lanes_a, 0)
    sent(send1, recv1, lanes_b, 1)
    sent(send1, recv1, lanes_c, 5, two)
    sent(send2, recv2, lanes_a, 2)
    sent(send2, recv2, lanes_b, 3)
    sent(send2, recv2, lanes_c, 6, two)
    pltpu.make_async_copy(part, parts_in, send_sem.at[4]).wait()
    to_sibling.wait_send()
    for k in range(2):
        to_across(k).wait_send()
        onward(k).wait_send()


def hand_over(sub_in, res_in, sub_out, res_out):
    sub_out[...] = sub_in[...]
    res_out[...] = res_in[...]


def local(coefficients, index_map, potential):
    tables = [jnp.asarray(t) for t in make_tables()]
    coef = coefficients.reshape(2, 128, 128)
    index = index_map.reshape(128, 128)
    inputs = (index, coef, potential, *tables)
    field = VMEM((SLAB, PARTS, LANES), F32)
    sub, res = pl.pallas_call(
        kernel,
        out_shape=(
            jax.ShapeDtypeStruct((2, 1, 4), F32),
            jax.ShapeDtypeStruct((2, 128, 128), F32),
        ),
        in_specs=[pl.BlockSpec(memory_space=pltpu.HBM)] * len(inputs),
        out_specs=[pl.BlockSpec(memory_space=VMEM)] * 2,
        scratch_shapes=[VMEM(x.shape, x.dtype) for x in inputs]
        + [
            pltpu.SemaphoreType.DMA((len(inputs),)),
            VMEM((SLAB, HALF, 384), F32),
            VMEM((SLAB, N, N), F32),
            VMEM((SLAB, 2, N, N), F32),
            VMEM((128, 128), F32),
            VMEM((128, 128), F32),
            VMEM((128, 128), F32),
            VMEM((128, 128), F32),
            VMEM((2, 128, 128), F32),
            VMEM((2, 128, 128), F32),
            VMEM((2, SLAB * HALF, 256), F32),
            field,
            field,
            field,
            field,
            VMEM((SLAB, 8, LANES), F32),
            VMEM((SLAB, PARTS, 128), F32),
            VMEM((4, 2, 128, 128), F32),
            VMEM((2, 128, 128), F32),
            VMEM((1, PARTS, 128), F32),
            VMEM((1, PARTS, 128), F32),
            pltpu.SemaphoreType.DMA((7,)),
            pltpu.SemaphoreType.DMA((7,)),
            pltpu.SemaphoreType.DMA((5,)),
            pltpu.SemaphoreType.DMA((5,)),
            pltpu.SemaphoreType.DMA,
        ],
        compiler_params=pltpu.CompilerParams(
            collective_id=0, has_side_effects=True, vmem_limit_bytes=56 << 20
        ),
        name="apply_potential",
    )(*inputs)
    sub, res = pl.pallas_call(
        hand_over,
        out_shape=(
            jax.ShapeDtypeStruct((2, 1, 4), F32),
            jax.ShapeDtypeStruct((2, 128, 128), F32),
        ),
        in_specs=[pl.BlockSpec(memory_space=VMEM), pl.BlockSpec(memory_space=VMEM)],
        out_specs=[pl.BlockSpec(memory_space=VMEM), pl.BlockSpec(memory_space=VMEM)],
        name="hand_over",
    )(sub, res)
    return sub.transpose(0, 2, 1), res.reshape(2, 1, 16384)


def solution(mesh):
    return jax.shard_map(
        local,
        mesh=mesh,
        in_specs=(P(None, "band", "grid"), P("grid"), P("grid", None)),
        out_specs=(P(None, None, "band"), P(None, "band", "grid")),
        check_vma=False,
    )
```

```python
import functools
import math

import jax
import jax.numpy as jnp
import ml_dtypes
import numpy as np
from jax import lax
from jax.experimental import pallas as pl
from jax.experimental.pallas import tpu as pltpu
from jax.sharding import PartitionSpec as P

N = 192
HALF = 96
PARTS = 64
SLAB = 3
KS = 64
KG = 128
LA, LB = 384, 256
LANES = LA + LB
F32, BF16 = jnp.float32, jnp.bfloat16
MESH = pl.DeviceIdType.MESH
VMEM = pltpu.VMEM


def split(table):
    hi = table.astype(np.float32).astype(ml_dtypes.bfloat16)
    lo = (table - hi.astype(np.float64)).astype(np.float32).astype(ml_dtypes.bfloat16)
    return hi, lo


def make_tables():
    turn = 2.0 * math.pi / N
    fold = np.arange(HALF)
    freq = np.where(fold < HALF // 2, fold, fold + HALF)
    plane = 3 * np.arange(PARTS)[None, :] + np.arange(SLAB)[:, None]
    plane = plane.reshape(-1)
    cells = np.arange(N)
    paired = np.concatenate([cells[0::2], cells[1::2]])
    angle = turn * (plane[:, None] * freq[None, :] % N)
    first = np.concatenate([np.cos(angle), np.sin(angle)], 0)
    angle = turn * (paired[:, None] * plane[None, :] % N)
    middle = np.concatenate([np.cos(angle), np.sin(angle)], 0)
    column = np.arange(HALF)
    column = np.where(column < 32, column, np.where(column < 64, column + 16, column))
    column[64:80] = np.arange(32, 48)
    col_freq = freq[column]
    lane_freq = np.zeros(256, np.int64)
    kind = np.full(256, -1)
    lane_freq[0:64], kind[0:64] = col_freq[:64], 0
    lane_freq[64:128], kind[64:128] = col_freq[:64], 1
    lane_freq[128:160], kind[128:160] = col_freq[64:], 0
    lane_freq[192:224], kind[192:224] = col_freq[64:], 1
    angle = turn * (lane_freq[:, None] * cells[None, :] % N)
    cos, sin = np.cos(angle), np.sin(angle)
    re, im = (kind == 0)[:, None], (kind == 1)[:, None]
    to_re = re * cos - im * sin
    to_im = re * sin + im * cos
    norm = 1.0 / float(N) ** 3
    from_re = (re * cos - im * sin).T * norm
    from_im = (re * sin + im * cos).T * norm
    angle = turn * (plane[:, None] * paired[None, :] % N)
    middle_back = np.concatenate([np.cos(angle), np.sin(angle)], 0)
    angle = turn * (freq[:, None] * plane[None, :] % N)
    first_back = np.concatenate([np.cos(angle), np.sin(angle)], 0)
    tables = (first, middle, to_re, to_im, from_re, from_im, middle_back, first_back)
    signed = np.where(fold < HALF // 2, fold, fold - HALF)
    moved = np.abs(signed) > 42
    home = np.where(moved, np.sign(signed) * (85 - np.abs(signed)), signed) % 85
    select = np.zeros((2, SLAB, HALF, 256), np.float32)
    for p in range(SLAB):
        for f in range(HALF):
            if f != HALF // 2:
                select[int(moved[f]), p, f, 85 * p + home[f]] = 1.0
    select = select.reshape(2, SLAB * HALF, 256).astype(ml_dtypes.bfloat16)
    row_fa = np.arange(256) % 85
    row_fa = np.where(row_fa < 43, row_fa, row_fa - 85)
    col_fc = signed[column]
    inside = row_fa[None, :] ** 2 + col_fc[:, None] ** 2 < (N // 4) ** 2
    return [np.stack(split(table)) for table in tables] + [select, inside.astype(np.float32)]


def halves(x):
    hi = x.astype(BF16)
    return hi, (x - hi.astype(F32)).astype(BF16)


def dot(a, b):
    return jnp.dot(a, b, preferred_element_type=F32)


def dot_left(table, hi, lo):
    return dot(table[0], hi) + dot(table[1], hi) + dot(table[0], lo)


def dot_right(hi, lo, table):
    return dot(hi, table[0]) + dot(lo, table[0]) + dot(hi, table[1])


def groups(x):
    return [x[:, 128 * g : 128 * g + 128] for g in range(x.shape[1] // 128)]


def combine(both, sign):
    rows = both.shape[0] // 2
    lane = lax.broadcasted_iota(jnp.int32, (rows, 128), 1)
    factor = jnp.where(lane < 64, -sign, sign).astype(F32)
    parts = [
        c + factor * pltpu.roll(s, 64, 1)
        for c, s in zip(groups(both[:rows]), groups(both[rows:]))
    ]
    return jnp.concatenate(parts, 1)


def kernel(
    index_hbm,
    coef_hbm,
    pot_hbm,
    first_hbm,
    middle_hbm,
    to_re_hbm,
    to_im_hbm,
    from_re_hbm,
    from_im_hbm,
    middle_back_hbm,
    first_back_hbm,
    select_hbm,
    inside_hbm,
    sub_ref,
    res_ref,
    index_ref,
    coef_ref,
    pot_flat,
    first,
    middle,
    to_re,
    to_im,
    from_re,
    from_im,
    middle_back,
    first_back,
    select,
    inside,
    load_sem,
    pot_rows,
    pot_ref,
    field_ref,
    row_key,
    col_key,
    row_home,
    col_home,
    coef_hi,
    coef_lo,
    acc,
    send1,
    recv1,
    send2,
    recv2,
    trash,
    last_plane,
    all_coef,
    applied,
    part,
    parts_in,
    send_sem,
    recv_sem,
    band_send,
    band_recv,
    own_sem,
):
    sources = (
        (index_hbm, index_ref),
        (coef_hbm, coef_ref),
        (first_hbm, first),
        (middle_hbm, middle),
        (to_re_hbm, to_re),
        (to_im_hbm, to_im),
        (pot_hbm, pot_flat),
        (from_re_hbm, from_re),
        (from_im_hbm, from_im),
        (middle_back_hbm, middle_back),
        (first_back_hbm, first_back),
        (select_hbm, select),
        (inside_hbm, inside),
    )
    loads = [
        pltpu.make_async_copy(src, dst, load_sem.at[k]) for k, (src, dst) in enumerate(sources)
    ]
    for load in loads:
        load.start()

    me = lax.axis_index("grid")
    band = lax.axis_index("band")
    sibling = band + 1 - 2 * lax.rem(band, 2)
    across = lax.rem(band + 2, 4)
    opposite = lax.rem(sibling + 2, 4)

    barrier = pltpu.get_barrier_semaphore()

    def greet(i):
        pl.semaphore_signal(
            barrier,
            inc=1,
            device_id={
                "grid": lax.rem(me + i, PARTS),
                "band": jnp.where(i == 0, sibling, band),
            },
            device_id_type=MESH,
        )

    pl.semaphore_signal(barrier, inc=1, device_id={"band": across}, device_id_type=MESH)

    loads[0].wait()
    loads[1].wait()
    cell = index_ref[...].astype(F32)
    line = jnp.floor((cell + 0.5) * (1.0 / N))
    gc = cell - N * line
    ga = jnp.floor((cell + 0.5) * (1.0 / (SLAB * N)))
    slab = line - SLAB * ga
    row_key[...] = slab * HALF + jnp.where(ga < HALF, ga, ga - HALF)
    fold = jnp.where(gc < HALF, gc, gc - HALF)
    col = jnp.where(fold < 32, fold, jnp.where(fold < 80, fold - 16, fold))
    col = jnp.where(jnp.logical_and(fold >= 32, fold < 48), fold + 32, col)
    col_key[...] = col
    fa = jnp.where(ga < HALF, ga, ga - N)
    moved = jnp.abs(fa) > 42
    home = jnp.where(moved, jnp.where(fa > 0, 85 - fa, -85 - fa), fa)
    row_home[...] = slab * 85 + jnp.where(home < 0, home + 85, home)
    turned = jnp.where(
        col < 64,
        jnp.where(col < 32, col + 32, col - 32),
        jnp.where(col < 80, col + 16, col - 16),
    )
    col_home[...] = jnp.where(moved, turned, col)
    coef = coef_ref[...]
    coef_hi[...] = coef.astype(BF16).astype(F32)
    coef_lo[...] = coef - coef.astype(BF16).astype(F32)
    acc[...] = jnp.zeros_like(acc)

    iota96 = lax.broadcasted_iota(jnp.int32, (HALF, 128), 0).astype(F32)
    iota96h = iota96.astype(BF16)
    one, zero = jnp.ones((), BF16), jnp.zeros((), BF16)
    zero32 = jnp.zeros((32, 128), BF16)

    def wide(x):
        return jnp.broadcast_to(x.astype(BF16), (HALF, 128))

    def row_hot(i):
        pieces = []
        for s in range(KS):
            key = row_key[pl.ds(i * KS + s, 1), :]
            pieces.append(
                jnp.concatenate(
                    [jnp.where(iota96h == wide(key - HALF * p), one, zero) for p in range(SLAB)], 0
                )
            )
        return jnp.concatenate(pieces, 1)

    iota256h = lax.broadcasted_iota(jnp.int32, (256, 128), 0).astype(F32).astype(BF16)

    def home_hot(i):
        pieces = []
        for s in range(KG):
            key = row_home[pl.ds(i * KG + s, 1), :].astype(BF16)
            pieces.append(jnp.where(iota256h == jnp.broadcast_to(key, (256, 128)), one, zero))
        return jnp.concatenate(pieces, 1)

    def scatter_step(low, count):
        pad = [] if count == 64 else [zero32]
        iota = iota96h[:count]

        def step(i, carry):
            pieces = []
            for s in range(KS):
                row = pl.ds(i * KS + s, 1)
                mask = iota == jnp.broadcast_to((col_key[row, :] - low).astype(BF16), (count, 128))
                blocks = []
                for ref in (coef_hi, coef_lo):
                    for k in range(2):
                        value = jnp.broadcast_to(ref[k, row, :].astype(BF16), (count, 128))
                        blocks += [jnp.where(mask, value, zero)] + pad
                pieces.append(jnp.concatenate(blocks, 0))
            acc[low // 64] += lax.dot_general(
                row_hot(i),
                jnp.concatenate(pieces, 1),
                (((1,), (1,)), ((), ())),
                preferred_element_type=F32,
            )
            return carry

        return step

    steps = 128 // KS
    early = scatter_step(0, 64)

    def early_step(i, carry):
        for k in range(2 * PARTS // steps):
            greet(i * (2 * PARTS // steps) + k)
        return early(i, carry)

    lax.fori_loop(0, steps // 2, early_step, 0)
    pl.semaphore_wait(barrier, PARTS - 1 + 2)

    def band_copy(src, dst, slot, to):
        return pltpu.make_async_remote_copy(
            src_ref=src,
            dst_ref=dst,
            send_sem=band_send.at[slot],
            recv_sem=band_recv.at[slot],
            device_id={"band": to},
            device_id_type=MESH,
        )

    def to_across(k):
        return band_copy(coef_ref.at[k], all_coef.at[band, k], k, across)

    def onward(k):
        return band_copy(all_coef.at[across, k], all_coef.at[across, k], 3 + k, sibling)

    to_sibling = band_copy(coef_ref, all_coef.at[band], 2, sibling)
    keep = pltpu.make_async_copy(coef_ref, all_coef.at[band], own_sem)
    to_across(0).start()
    to_sibling.start()
    keep.start()
    lax.fori_loop(steps // 2, steps, scatter_step(0, 64), 0)

    def exchange(src, dst, own, lanes, slot):
        def one_copy(i, carry):
            peer = lax.rem(me + i, PARTS)
            pltpu.make_async_remote_copy(
                src_ref=src.at[own, peer, lanes],
                dst_ref=dst.at[own, me, lanes],
                send_sem=send_sem.at[slot],
                recv_sem=recv_sem.at[slot],
                device_id={"grid": peer},
                device_id_type=MESH,
            ).start()
            return carry

        lax.fori_loop(1, PARTS, one_copy, 0)
        pltpu.make_async_copy(
            src.at[own, me, lanes], dst.at[own, me, lanes], recv_sem.at[slot]
        ).start()
        pltpu.make_async_copy(
            src.at[own, me, lanes], trash.at[own, slot, lanes], send_sem.at[slot]
        ).start()

    def arrive(src, dst, lanes, slot, own=pl.ds(0, SLAB)):
        pltpu.make_async_copy(
            src.at[own, :, lanes], dst.at[own, :, lanes], recv_sem.at[slot]
        ).wait()

    def sent(src, dst, lanes, slot, own=pl.ds(0, SLAB)):
        pltpu.make_async_copy(
            src.at[own, :, lanes], dst.at[own, :, lanes], send_sem.at[slot]
        ).wait()

    lanes_a, lanes_b, lanes_c = pl.ds(0, LA), pl.ds(LA, 128), pl.ds(LA + 128, 128)
    every, two = pl.ds(0, SLAB), pl.ds(0, 2)

    def spectrum_a(offset):
        a = [acc[0, HALF * p : HALF * p + HALF, offset : offset + 128] for p in range(SLAB)]
        return jnp.concatenate(a, 1).astype(BF16)

    def spectrum_b(offset):
        b = [acc[1, HALF * p : HALF * p + HALF, offset : offset + 128] for p in range(SLAB)]
        return jnp.concatenate([b[0] + pltpu.roll(b[1], 32, 1), b[2]], 1).astype(BF16)

    loads[2].wait()
    out = combine(dot_left(first, spectrum_a(0), spectrum_a(128)), 1.0)
    for j in range(SLAB):
        send1[j, :, 0:LA] = out[PARTS * j : PARTS * j + PARTS]
    exchange(send1, recv1, every, lanes_a, 0)
    lax.fori_loop(0, steps, scatter_step(64, 32), 0)
    out = combine(dot_left(first, spectrum_b(0), spectrum_b(128)), 1.0)
    for j in range(SLAB):
        send1[j, :, LA : LA + 128] = out[PARTS * j : PARTS * j + PARTS, 0:128]
    send1[0, :, 512:640] = out[0:64, 128:256] + pltpu.roll(out[64:128, 128:256], 32, 1)
    send1[1, :, 512:640] = out[128:192, 128:256]
    exchange(send1, recv1, every, lanes_b, 1)
    exchange(send1, recv1, two, lanes_c, 5)

    band_copy(coef_ref.at[0], all_coef.at[across, 0], 0, across).wait_recv()
    onward(0).start()

    for load in loads[3:]:
        load.wait()

    def pot_row(q, carry):
        both = pot_flat[:, pl.ds(pl.multiple_of(q * 384, 128), 384)]
        for j in range(SLAB):
            pot_rows[j, pl.ds(q, 1), :] = both[j : j + 1]
        return carry

    lax.fori_loop(0, HALF, pot_row, 0)
    for j in range(SLAB):
        pot_ref[j, 0:HALF] = pot_rows[j, :, 0:N]
        pot_ref[j, HALF:N] = pltpu.roll(pot_rows[j], N, 1)[:, 0:N]

    arrive(send1, recv1, lanes_a, 0)

    def middle_a(j, carry):
        x = recv1[j, :, 0:LA]
        x = jnp.concatenate([x[:, 0:128], x[:, 128:256], x[:, 256:384]], 0)
        hi, lo = halves(combine(dot_left(middle, *halves(x)), 1.0))
        field_ref[j, 0] = dot_right(hi, lo, to_re[:, 0:128])
        field_ref[j, 1] = dot_right(hi, lo, to_im[:, 0:128])
        return carry

    lax.fori_loop(0, SLAB, middle_a, 0)
    arrive(send1, recv1, lanes_b, 1)
    arrive(send1, recv1, lanes_c, 5, two)

    def middle_b(j, carry):
        x = recv1[j, :, LA : LA + 128]
        y = recv1[j // 2, :, 512:640]
        y = jnp.where(j == 1, pltpu.roll(y, 96, 1), y)
        x = jnp.concatenate([x, pltpu.roll(x, 96, 1), y], 0)
        hi, lo = halves(combine(dot_left(middle, *halves(x)), 1.0))
        pot = pot_ref[j]
        field_re = (field_ref[j, 0] + dot_right(hi, lo, to_re[:, 128:256])) * pot
        field_im = (field_ref[j, 1] + dot_right(hi, lo, to_im[:, 128:256])) * pot
        x = dot_right(*halves(field_re), from_re) + dot_right(*halves(field_im), from_im)
        x = combine(dot_left(middle_back, *halves(x)), -1.0)
        for p in range(SLAB):
            send2[j, :, 128 * p : 128 * p + 128] = x[PARTS * p : PARTS * p + PARTS, 0:128]
        send2[j, :, 384:512] = x[0:64, 128:256] + pltpu.roll(x[64:128, 128:256], 32, 1)
        last_plane[j] = x[128:192, 128:256]
        exchange(send2, recv2, pl.ds(j, 1), lanes_a, 2)
        return carry

    to_across(1).start()
    lax.fori_loop(0, SLAB, middle_b, 0)
    exchange(send2, recv2, every, lanes_b, 3)
    send2[0, :, 512:640] = last_plane[0] + pltpu.roll(last_plane[1], 32, 1)
    send2[1, :, 512:640] = last_plane[2]
    exchange(send2, recv2, two, lanes_c, 6)

    def gather(low, count):
        def rows_of(x):
            if low == 0:
                return [x[:, 0:128], x[:, 128:256], x[:, 256:384]]
            return [x[:, 0:128], pltpu.roll(x[:, 0:128], 96, 1), x[:, 128:256]]

        if low == 0:
            x = recv2[:, :, 0:LA].reshape(N, LA)
        else:
            y = recv2[0, :, 512:640]
            y = jnp.concatenate([y, pltpu.roll(y, 96, 1), recv2[1, :, 512:640]], 0)
            x = jnp.concatenate([recv2[:, :, LA : LA + 128].reshape(N, 128), y], 1)
        x = combine(dot_left(first_back, *halves(x)), -1.0)
        x = jnp.concatenate(rows_of(x), 0).T
        hi, lo = halves(jnp.concatenate([x[0:count], x[64 : 64 + count]], 0))
        table = jnp.concatenate([hi, lo], 0)
        turned = []
        for k in range(4):
            block = table[count * k : count * k + count]
            turned += [block[count // 2 :], block[: count // 2]]
        keep_own = inside[low : low + count, :]
        table = jnp.where(
            jnp.concatenate([keep_own] * 4, 0) > 0.5,
            dot(table, select[0]),
            dot(jnp.concatenate(turned, 0), select[1]),
        ).astype(BF16)
        iota = iota96[:count]

        def step(i, carry):
            found = dot(table, home_hot(i))
            found = found[: 2 * count] + found[2 * count :]
            for s in range(KG):
                row = pl.ds(i * KG + s, 1)
                mask = iota == jnp.broadcast_to(col_home[row, :] - low, (count, 128))
                here = found[:, 128 * s : 128 * s + 128]
                for k in range(2):
                    kept = jnp.where(mask, here[count * k : count * k + count], 0.0)
                    kept = kept.reshape(count // 8, 8, 128).sum(0).sum(0, keepdims=True)
                    applied[k, row, :] = kept if low == 0 else applied[k, row, :] + kept
            return carry

        lax.fori_loop(0, 128 // KG, step, 0)

    band_copy(coef_ref.at[1], all_coef.at[across, 1], 1, across).wait_recv()
    onward(1).start()
    arrive(send2, recv2, lanes_a, 2)
    gather(0, 64)
    arrive(send2, recv2, lanes_b, 3)
    arrive(send2, recv2, lanes_c, 6, two)
    gather(64, 32)

    band_copy(coef_ref, all_coef.at[sibling], 2, sibling).wait_recv()
    for k in range(2):
        band_copy(coef_ref.at[k], all_coef.at[opposite, k], 3 + k, sibling).wait_recv()
    keep.wait()

    h_re, h_im = applied[0], applied[1]
    sums = []
    for i in range(4):
        c_re, c_im = all_coef[i, 0], all_coef[i, 1]
        sums.append((c_re * h_re + c_im * h_im, c_re * h_im - c_im * h_re))
    lanes = [s[0].sum(0, keepdims=True) for s in sums] + [s[1].sum(0, keepdims=True) for s in sums]
    total = jnp.concatenate(lanes, 0).sum(1, keepdims=True)
    eye = lax.broadcasted_iota(jnp.int32, (8, 128), 0) == lax.broadcasted_iota(
        jnp.int32, (8, 128), 1
    )
    line = jnp.where(eye, jnp.broadcast_to(total, (8, 128)), 0.0).sum(0, keepdims=True)
    part[...] = jnp.broadcast_to(line.reshape(1, 1, 128), part.shape)

    def share(i, carry):
        peer = lax.rem(me + i, PARTS)
        pltpu.make_async_remote_copy(
            src_ref=part.at[:, 0],
            dst_ref=parts_in.at[:, me],
            send_sem=send_sem.at[4],
            recv_sem=recv_sem.at[4],
            device_id={"grid": peer},
            device_id_type=MESH,
        ).start()
        return carry

    lax.fori_loop(1, PARTS, share, 0)
    pltpu.make_async_copy(part.at[:, 0], parts_in.at[:, me], recv_sem.at[4]).start()
    pltpu.make_async_copy(part.at[:, 0], trash.at[pl.ds(0, 1), 4, pl.ds(0, 128)], send_sem.at[4]).start()
    pltpu.make_async_copy(part, parts_in, recv_sem.at[4]).wait()

    line = parts_in[0].sum(0, keepdims=True) * (1.0 / (PARTS * 16384))
    sub_ref[0] = line[:, 0:4]
    sub_ref[1] = line[:, 4:8]
    r_re, r_im = h_re, h_im
    for i in range(4):
        s_re = jnp.broadcast_to(line[:, i : i + 1], (128, 128))
        s_im = jnp.broadcast_to(line[:, i + 4 : i + 5], (128, 128))
        c_re, c_im = all_coef[i, 0], all_coef[i, 1]
        r_re = r_re - (c_re * s_re - c_im * s_im)
        r_im = r_im - (c_re * s_im + c_im * s_re)
    res_ref[0] = r_re
    res_ref[1] = r_im

    sent(send1, recv1, lanes_a, 0)
    sent(send1, recv1, lanes_b, 1)
    sent(send1, recv1, lanes_c, 5, two)
    sent(send2, recv2, lanes_a, 2)
    sent(send2, recv2, lanes_b, 3)
    sent(send2, recv2, lanes_c, 6, two)
    pltpu.make_async_copy(part, parts_in, send_sem.at[4]).wait()
    to_sibling.wait_send()
    for k in range(2):
        to_across(k).wait_send()
        onward(k).wait_send()


def hand_over(sub_in, res_in, sub_out, res_out):
    sub_out[...] = sub_in[...]
    res_out[...] = res_in[...]


def local(coefficients, index_map, potential):
    tables = [jnp.asarray(t) for t in make_tables()]
    coef = coefficients.reshape(2, 128, 128)
    index = index_map.reshape(128, 128)
    inputs = (index, coef, potential, *tables)
    field = VMEM((SLAB, PARTS, LANES), F32)
    sub, res = pl.pallas_call(
        kernel,
        out_shape=(
            jax.ShapeDtypeStruct((2, 1, 4), F32),
            jax.ShapeDtypeStruct((2, 128, 128), F32),
        ),
        in_specs=[pl.BlockSpec(memory_space=pltpu.HBM)] * len(inputs),
        out_specs=[pl.BlockSpec(memory_space=VMEM)] * 2,
        scratch_shapes=[VMEM(x.shape, x.dtype) for x in inputs]
        + [
            pltpu.SemaphoreType.DMA((len(inputs),)),
            VMEM((SLAB, HALF, 384), F32),
            VMEM((SLAB, N, N), F32),
            VMEM((SLAB, 2, N, N), F32),
            VMEM((128, 128), F32),
            VMEM((128, 128), F32),
            VMEM((128, 128), F32),
            VMEM((128, 128), F32),
            VMEM((2, 128, 128), F32),
            VMEM((2, 128, 128), F32),
            VMEM((2, SLAB * HALF, 256), F32),
            field,
            field,
            field,
            field,
            VMEM((SLAB, 8, LANES), F32),
            VMEM((SLAB, PARTS, 128), F32),
            VMEM((4, 2, 128, 128), F32),
            VMEM((2, 128, 128), F32),
            VMEM((1, PARTS, 128), F32),
            VMEM((1, PARTS, 128), F32),
            pltpu.SemaphoreType.DMA((7,)),
            pltpu.SemaphoreType.DMA((7,)),
            pltpu.SemaphoreType.DMA((5,)),
            pltpu.SemaphoreType.DMA((5,)),
            pltpu.SemaphoreType.DMA,
        ],
        compiler_params=pltpu.CompilerParams(
            collective_id=0, has_side_effects=True, vmem_limit_bytes=56 << 20
        ),
        name="apply_potential",
    )(*inputs)
    sub, res = pl.pallas_call(
        hand_over,
        out_shape=(
            jax.ShapeDtypeStruct((2, 1, 4), F32),
            jax.ShapeDtypeStruct((2, 128, 128), F32),
        ),
        in_specs=[pl.BlockSpec(memory_space=VMEM), pl.BlockSpec(memory_space=VMEM)],
        out_specs=[pl.BlockSpec(memory_space=VMEM), pl.BlockSpec(memory_space=VMEM)],
        name="hand_over",
    )(sub, res)
    return sub.transpose(0, 2, 1), res.reshape(2, 1, 16384)


def solution(mesh):
    return jax.shard_map(
        local,
        mesh=mesh,
        in_specs=(P(None, "band", "grid"), P("grid"), P("grid", None)),
        out_specs=(P(None, None, "band"), P(None, "band", "grid")),
        check_vma=False,
    )
```
